256 devices in a mesh: rep: 4 (over z_lo), fsdp: 64 (over x, z_hi, y, core).
Axes of the slice: x: 4, y: 4, z: 8 (z_hi: 2, z_lo: 4; z = z_hi * 4 + z_lo), core: 2. Of those that a mesh axis runs over, the one named last changes fastest.
Arguments:
- latents: bfloat16 [256, 16, 16, 640], P(('rep', 'fsdp')), may hold values from -6 to 6
- cotangent: bfloat16 [256, 16, 16, 640], P(('rep', 'fsdp')), may hold values from -6 to 6
- conv_weight: bfloat16 [4, 5760, 640], P('rep', 'fsdp'), may hold values from -0.078125 to 0.078125
- norm_gain: float32 [4, 640], P('rep'), may hold values from 0.5 to 1.5
- norm_shift: float32 [4, 640], P('rep'), may hold values from -3 to 3
- partner_bit: int32 [64], replicated, may hold values from 0 to 1
Outputs:
- block_out: bfloat16 [256, 16, 16, 640], P(('rep', 'fsdp'))
- input_grad: bfloat16 [256, 16, 16, 640], P(('rep', 'fsdp'))
- weight_grad: float32 [4, 5760, 640], P('rep', 'fsdp')
- norm_grad: float32 [4, 2, 640], P('rep')
The draws below stay inside these ranges and needn't reach their ends.
Inputs may be any that keep to these rules, and one draw needn't show every extreme that they name: In row shard f, replica r is paired with replica r with bit partner_bit[f] of its index flipped.
All inputs are finite; a program needn't handle non-finite values.
Results may differ from the reference program's by a relative error of at most 0.0065.
Values may be sent and summed in bfloat16 or wider, within the bound.
A program may use at most 128 MiB of HBM per device.

```python
import jax
import jax.numpy as jnp
from jax import lax

C = 640
GROUPS = 32
HW = 16
LAT = 1
KROWS = 5760
BATCH = 256
N_REP = 4
N_FSDP = 64


def place_ends(values, key, low, top_value):
    longest = values.shape.index(max(values.shape))
    spots = []
    for shift in (0, 1):
        where = [jax.random.randint(jax.random.fold_in(key, axis), (), 0, length) for axis, length in enumerate(values.shape)]
        where[longest] = (where[longest] + shift) % values.shape[longest]
        spots.append(tuple(where))
    return values.at[spots[0]].set(low).at[spots[1]].set(top_value)


def block_scale(stream_key, shape, cuts, low, top_value):
    factor_of = 1.0
    for position, blocks in cuts:
        draws = jax.random.uniform(jax.random.fold_in(jax.random.fold_in(stream_key, 6), position), (blocks,), jnp.float32, low / len(cuts), top_value / len(cuts))
        factor_of = factor_of * jnp.repeat(jnp.exp(draws), shape[position] // blocks).reshape((-1,) + (1,) * (len(shape) - 1 - position))
    return factor_of


def normal_values(own_key, shape, scale, reach, cuts=(), kind=jnp.bfloat16):
    values = scale * jax.random.normal(own_key, shape, jnp.float32)
    if cuts:
        values = values * block_scale(own_key, shape, cuts, -0.22, 0.18)
    return jnp.clip(values, -reach, reach).astype(kind)


def setup_inputs(seed: int = 0) -> dict:
    arg_keys = jax.random.split(jax.random.key(seed), 7)
    return {
        "latents": normal_values(arg_keys[0], (BATCH, HW, HW, C), 1.0, 6.0, ((0, 256),)),
        "cotangent": normal_values(arg_keys[1], (BATCH, HW, HW, C), 1.0, 6.0, ((0, 256),)),
        "conv_weight": normal_values(arg_keys[2], (N_REP, KROWS, C), KROWS ** -0.5, 0.078125, ((0, 4), (1, 64))),
        "norm_gain": jnp.clip(0.5 + 1.0 * jax.random.uniform(arg_keys[3], (N_REP, C), jnp.float32) ** block_scale(arg_keys[3], (N_REP, C), ((0, 4),), -0.2, 0.2), 0.5, 1.5),
        "norm_shift": normal_values(arg_keys[4], (N_REP, C), 0.5, 3.0, ((0, 4),), jnp.float32),
        "partner_bit": place_ends(jax.random.randint(arg_keys[5], (N_FSDP,), 0, 2), jax.random.fold_in(arg_keys[5], 1), 0, 1).astype(jnp.int32),
    }


def norm_forward(values_in, gain, shift, groups):
    count, side, chans = (values_in.shape[0], values_in.shape[1], values_in.shape[3])
    values = values_in.astype(jnp.float32).reshape(count, side * side, groups, chans // groups)
    center = lax.optimization_barrier(jnp.mean(values, axis=(1, 3), keepdims=True))
    spread = lax.optimization_barrier(jnp.mean(jnp.square(values - center), axis=(1, 3), keepdims=True))
    scale_inv = lax.rsqrt(spread + 1e-05)
    normed = (values - center) * scale_inv
    pre_act = normed * gain.reshape(groups, -1) + shift.reshape(groups, -1)
    return (normed, scale_inv, pre_act)

def make_patches(activation):
    count, side, chans = (activation.shape[0], activation.shape[1], activation.shape[3])
    padded = jnp.pad(activation, ((0, 0), (1, 1), (1, 1), (0, 0)))
    pieces = [padded[:, row_off:row_off + side, col_off:col_off + side, :] for row_off in range(3) for col_off in range(3)]
    return jnp.concatenate(pieces, axis=-1).reshape(count * side * side, 9 * chans)

def fold_patches(patch_grad, count, side, chans):
    grads = patch_grad.reshape(count, side, side, 9, chans)
    total = jnp.zeros((count, side + 2, side + 2, chans), jnp.float32)
    for row_off in range(3):
        for col_off in range(3):
            tap = grads[:, :, :, row_off * 3 + col_off, :]
            total = total + jnp.pad(tap, ((0, 0), (row_off, 2 - row_off), (col_off, 2 - col_off), (0, 0)))
    return total[:, 1:-1, 1:-1, :]

def backward_rest(act_grad, normed, scale_inv, pre_act, gain, groups, inv_batch):
    count, side, chans = (act_grad.shape[0], act_grad.shape[1], act_grad.shape[3])
    act_grad = act_grad.reshape(count, side * side, groups, chans // groups)
    sigma = jax.nn.sigmoid(pre_act)
    pre_grad = act_grad * sigma * (1.0 + pre_act * (1.0 - sigma))
    gain_grad = lax.optimization_barrier(jnp.sum(pre_grad * normed, axis=(0, 1))).reshape(-1) * inv_batch
    shift_grad = lax.optimization_barrier(jnp.sum(pre_grad, axis=(0, 1))).reshape(-1) * inv_batch
    normed_grad = pre_grad * gain.reshape(groups, -1)
    first = lax.optimization_barrier(jnp.mean(normed_grad, axis=(1, 3), keepdims=True))
    second = lax.optimization_barrier(jnp.mean(normed_grad * normed, axis=(1, 3), keepdims=True))
    input_grad = scale_inv * (normed_grad - first - normed * second)
    return (input_grad.reshape(count, side, side, chans).astype(jnp.bfloat16), jnp.stack([gain_grad, shift_grad]))

def local_block(block_in, block_cot, weights, gain, shift, inv_batch):
    count, side, chans = (block_in.shape[0], block_in.shape[1], block_in.shape[3])
    normed, scale_inv, pre_act = norm_forward(block_in, gain, shift, GROUPS)
    activation = jax.nn.silu(pre_act).astype(jnp.bfloat16).reshape(count, side, side, chans)
    patches = make_patches(activation)
    cot_rows = block_cot.reshape(count * side * side, chans)
    output = jnp.dot(patches, weights, preferred_element_type=jnp.float32).astype(jnp.bfloat16)
    patch_grad = lax.dot_general(cot_rows, weights, (((1,), (1,)), ((), ())), preferred_element_type=jnp.float32)
    act_grad = fold_patches(patch_grad, count, side, chans)
    input_grad, norm_term = backward_rest(act_grad, normed, scale_inv, pre_act, gain, GROUPS, inv_batch)
    weight_term = lax.dot_general(patches, cot_rows, (((0,), (0,)), ((), ())), preferred_element_type=jnp.float32) * inv_batch
    return (output.reshape(count, side, side, chans), input_grad, weight_term, norm_term)

def reference(latents, cotangent, conv_weight, norm_gain, norm_shift, partner_bit):
    inv_batch = 1.0 / (LAT * N_FSDP)
    shaped_in = latents.reshape(N_REP, N_FSDP, LAT, HW, HW, C)
    shaped_cot = cotangent.reshape(N_REP, N_FSDP, LAT, HW, HW, C)

    def replica(items):
        rep_in, rep_cot, weights, gain, shift = items

        def step(carry, block):
            weight_acc, norm_acc = carry
            output, input_grad, weight_term, norm_term = local_block(block[0], block[1], weights, gain, shift, inv_batch)
            return ((weight_acc + weight_term, norm_acc + norm_term), (output, input_grad))
        start = (jnp.zeros((KROWS, C), jnp.float32), jnp.zeros((2, C), jnp.float32))
        (weight_sum, norm_sum), (outputs, grads) = lax.scan(step, start, (rep_in, rep_cot))
        return (outputs, grads, weight_sum, norm_sum)
    outputs, grads, weight_sums, norm_sums = lax.map(replica, (shaped_in, shaped_cot, conv_weight, norm_gain, norm_shift))
    replica_ids = jnp.arange(N_REP, dtype=jnp.int32)
    shard_ids = jnp.arange(N_FSDP, dtype=jnp.int32)
    flips = jnp.left_shift(jnp.int32(1), partner_bit.astype(jnp.int32))
    partners = jnp.bitwise_xor(replica_ids[:, None], flips[None, :])
    shaped_weight = weight_sums.reshape(N_REP, N_FSDP, KROWS // N_FSDP, C)
    partner_weight = shaped_weight[partners, shard_ids[None, :]]
    weight_grad = (0.5 * (shaped_weight + partner_weight)).reshape(N_REP, KROWS, C)
    norm_partner = jnp.bitwise_xor(replica_ids, flips[0])
    norm_grad = 0.5 * (norm_sums + jnp.take(norm_sums, norm_partner, axis=0))
    block_out = outputs.reshape(BATCH, HW, HW, C)
    input_grad = grads.reshape(BATCH, HW, HW, C)
    return (block_out, input_grad, weight_grad, norm_grad)
```

```python
import jax
import jax.numpy as jnp
from jax import lax
from jax.experimental import pallas as pl
from jax.experimental.pallas import tpu as pltpu
from jax.sharding import PartitionSpec as P

GROUPS = 32
SIDE = 16
POS = SIDE * SIDE
SLAB = 96
UNROLL = 4
BF = jnp.bfloat16
F32 = jnp.float32
TAPS = [(a - 1, b - 1) for a in range(3) for b in range(3)]


def order(step):
    return (step + (step // 2) * (1 - 2 * (step % 2)) + 2) % 4


def lane_mask(down, right):
    lane = lax.broadcasted_iota(jnp.int32, (1, POS), 1)
    row, col = lane // SIDE + down, lane % SIDE + right
    return (row >= 0) & (row < SIDE) & (col >= 0) & (col < SIDE)


def kernel(
    lat, cot, w_in, gain, shift, bits, out, in_grad, w_grad, n_grad,
    wg, pt, tall, cs, tm, bacc, xt, nt, at, acc, gcol, scol, rcol, ncol, fin,
    sib_s, sib_r, b2_s, b2_r, b1_s, b1_r, a2_s, a2_r, a1_s, a1_r, z_s, z_r, p_s, p_r,
    n1_s, n1_r, n2_s, n2_r, n3_s, n3_r,
    ag_ss, ag_rs, sib_ss, sib_rs, b2_ss, b2_rs, b1_ss, b1_rs, a2_ss, a2_rs, a1_ss, a1_rs,
    z_ss, z_rs, p_ss, p_rs, n1_ss, n1_rs, n2_ss, n2_rs, n3_ss, n3_rs,
):
    chans = lat.shape[1]
    shard = w_in.shape[0]
    count = wg.shape[0]
    krows = count * shard
    rep, fs = lax.axis_index("rep"), lax.axis_index("fsdp")
    x, z, y, core = fs // 16, (fs // 8) % 2, (fs // 2) % 4, fs % 2
    a, b = x + (y - x) * core, y + (x - y) * core

    def slot(a_, z_, b_, core_):
        return (a_ % 4) * (16 - 14 * core_) + z_ * 8 + (b_ % 4) * (2 + 14 * core_) + core_

    def at_ab(da, db):
        return (rep, slot(a + da, z, b + db, core))

    sibling = (rep, fs + 1 - 2 * core)
    opposite = (rep, slot(a, 1 - z, b, core))
    partners = ((rep + 1 - 2 * (rep % 2), fs), (rep + 2 - 4 * (rep // 2), fs))

    def remote(src, dst, send_sem, recv_sem, device):
        return pltpu.make_async_remote_copy(
            src_ref=src, dst_ref=dst, send_sem=send_sem, recv_sem=recv_sem,
            device_id=device, device_id_type=pl.DeviceIdType.MESH,
        )

    sent = []

    def ag_send(index, *devices):
        for device in devices:
            copy = remote(wg.at[index], wg.at[index], ag_ss.at[len(sent)], ag_rs.at[index], device)
            copy.start()
            sent.append(copy)

    def ag_wait(index):
        remote(wg.at[index], wg.at[index], ag_ss.at[0], ag_rs.at[index], sibling).wait_recv()

    b_both = (at_ab(0, 1), at_ab(0, 3))
    a_both = (at_ab(1, 0), at_ab(3, 0))
    arrivals = [(0, z), (3, z), (1, z), (0, 1 - z), (2, z), (3, 1 - z), (1, 1 - z), (2, 1 - z)]

    def ag_first():
        ag_send(fs, *a_both, opposite, *b_both, sibling)

    def ag_near(zz):
        ag_wait(slot(a + 3, zz, b, core))
        ag_wait(slot(a + 1, zz, b, core))
        ag_send(slot(a + 3 + 2 * zz, zz, b, core), at_ab(1 + 2 * zz, 0))
        ag_send(slot(a + 3, zz, b, core), *b_both, sibling)
        ag_send(slot(a + 1, zz, b, core), *b_both, sibling)

    def ag_opposite():
        own = slot(a, 1 - z, b, core)
        ag_wait(own)
        ag_send(own, *a_both, *b_both, sibling)

    def ag_far(zz):
        own = slot(a + 2, zz, b, core)
        ag_wait(own)
        ag_send(own, *b_both, sibling)

    def ag_b(step):
        da, zz = arrivals[step]
        for db in (3, 1):
            ag_wait(slot(a + da, zz, b + db, core))
        ag_send(slot(a + da, zz, b + 3 + 2 * zz, core), at_ab(0, 1 + 2 * zz))
        for db in (3, 1):
            ag_send(slot(a + da, zz, b + db, core), sibling)

    def ag_b_far(step):
        da, zz = arrivals[step]
        own = slot(a + da, zz, b + 2, core)
        ag_wait(own)
        ag_send(own, sibling)

    def ag_sibling():
        def body(step, carry):
            ag_wait(2 * step + 1 - core)
            return carry

        lax.fori_loop(0, count // 2, body, 0)

    def plane(i):
        return z + (1 - 2 * z) * (1 - i // 4)

    def terms(first, indices):
        lhs = jnp.concatenate([pt[index] for index in indices], axis=0)
        return jnp.dot(lhs, cot[...], preferred_element_type=F32)

    def sib_copy(i):
        return remote(sib_s.at[i], sib_r.at[i], sib_ss.at[i], sib_rs.at[i], sibling)

    def sibling_terms(g):
        todo = [(i, jb) for i in (2 * g, 2 * g + 1) for jb in range(4)]
        value = terms(g, [slot(b + order(i % 4), plane(i), a + order(jb), 1 - core) for i, jb in todo])
        for n, (i, jb) in enumerate(todo):
            sib_s[i, jb] = value[n * SLAB : (n + 1) * SLAB].astype(BF)
            if jb == 3:
                sib_copy(i).start()

    def own_terms(g):
        todo = [(i, jb) for i in (2 * g, 2 * g + 1) for jb in range(4)]
        value = terms(g, [slot(a + order(i % 4), plane(i), b + order(jb), core) for i, jb in todo])
        for n, (i, jb) in enumerate(todo):
            tm[i, jb] = value[n * SLAB : (n + 1) * SLAB]

    def chip_term(i, jb):
        return tm[i, jb] + sib_r[i, jb].astype(F32)

    def b2_copy(i):
        return remote(b2_s.at[i], b2_r.at[i], b2_ss.at[i], b2_rs.at[i], at_ab(0, 1 + 2 * (i % 2)))

    def b1_copy(i, way):
        return remote(
            b1_s.at[i, way], b1_r.at[i, way], b1_ss.at[i, way], b1_rs.at[i, way],
            at_ab(0, 1 + 2 * way),
        )

    def rs_far(i):
        sib_copy(i).wait_recv()
        b2_s[i] = chip_term(i, 0).astype(BF)
        b2_copy(i).start()

    def rs_near(i):
        way = 1 - i % 2
        b1_s[i, way] = chip_term(i, 2 - way).astype(BF)
        b1_copy(i, way).start()

    def rs_late(i):
        way = i % 2
        b2_copy(i).wait_recv()
        b1_s[i, way] = (chip_term(i, 2 - way) + b2_r[i].astype(F32)).astype(BF)
        b1_copy(i, way).start()

    def row_term(i):
        for way in range(2):
            b1_copy(i, way).wait_recv()
        return chip_term(i, 3) + b1_r[i, 0].astype(F32) + b1_r[i, 1].astype(F32)

    def a2_copy(h):
        return remote(a2_s.at[h], a2_r.at[h], a2_ss.at[h], a2_rs.at[h], at_ab(1 + 2 * h, 0))

    def a1_copy(h, way):
        return remote(
            a1_s.at[h, way], a1_r.at[h, way], a1_ss.at[h, way], a1_rs.at[h, way],
            at_ab(1 + 2 * way, 0),
        )

    def rs_a_far(h):
        a2_s[h] = row_term(4 * h).astype(BF)
        a2_copy(h).start()

    def rs_a_near(h):
        way = 1 - h
        a1_s[h, way] = row_term(4 * h + 2 - way).astype(BF)
        a1_copy(h, way).start()

    def rs_a_late(h):
        way = h
        value = row_term(4 * h + 2 - way)
        a2_copy(h).wait_recv()
        a1_s[h, way] = (value + a2_r[h].astype(F32)).astype(BF)
        a1_copy(h, way).start()

    def plane_term(h):
        value = row_term(4 * h + 3)
        for way in range(2):
            a1_copy(h, way).wait_recv()
        return value + a1_r[h, 0].astype(F32) + a1_r[h, 1].astype(F32)

    z_copy = remote(z_s, z_r, z_ss, z_rs, opposite)
    p_copies = [remote(p_s, p_r.at[i], p_ss.at[i], p_rs.at[i], partners[i]) for i in range(2)]

    def rs_other_plane():
        z_s[...] = plane_term(0).astype(BF)
        z_copy.start()

    def rs_own_plane():
        value = plane_term(1)
        z_copy.wait_recv()
        value = value + z_r[...].astype(F32)
        fin[...] = value
        p_s[...] = value.astype(BF)
        for copy in p_copies:
            copy.start()

    def picked(index, first, second):
        second_share = bits[index].astype(F32)
        return first * (1.0 - second_share) + second * second_share

    def rs_partner():
        for copy in p_copies:
            copy.wait_recv()
        other = picked(fs, p_r[0].astype(F32), p_r[1].astype(F32))
        w_grad[...] = ((fin[...] + other) * (0.5 / count))[:shard].reshape(w_grad.shape)

    me1, me2 = x * 2 + core, z * 4 + y

    def peer1(d):
        other = (me1 + d) % 8
        return other, (rep, (other // 2) * 16 + z * 8 + y * 2 + other % 2)

    def peer2(d):
        other = (me2 + d) % 8
        return other, (rep, x * 16 + (other // 4) * 8 + (other % 4) * 2 + core)

    norm_stages = [(n1_s, n1_r, n1_ss, n1_rs, me1, peer1), (n2_s, n2_r, n2_ss, n2_rs, me2, peer2)]

    def norm_copy(stage, d, mine):
        send, recv, send_sems, recv_sems, me, peer = norm_stages[stage]
        other, device = peer(d)
        index = me if mine else other
        return remote(send, recv.at[index], send_sems.at[d], recv_sems.at[index], device)

    def norm_start(stage, value):
        send, recv, _, _, me, _ = norm_stages[stage]
        send[...] = value
        recv[me] = value
        for d in range(1, 8):
            norm_copy(stage, d, True).start()

    def norm_sum(stage):
        for d in range(1, 8):
            norm_copy(stage, d, False).wait_recv()
        recv = norm_stages[stage][1]
        total = recv[0]
        for i in range(1, 8):
            total = total + recv[i]
        return total

    n3_copies = [remote(n3_s, n3_r.at[i], n3_ss.at[i], n3_rs.at[i], partners[i]) for i in range(2)]

    def norm_partner_start():
        n3_s[...] = norm_sum(1)
        for copy in n3_copies:
            copy.start()

    def norm_last():
        for copy in n3_copies:
            copy.wait_recv()
        other = picked(0, n3_r[0], n3_r[1])
        n_grad[...] = ((n3_s[...] + other) * (0.5 / count))[:2]

    block = 40
    half = block // 2
    blocks = chans // block
    width = float(POS * (chans // GROUPS))

    def group_mean(column):
        first = lax.broadcasted_iota(jnp.int32, (block, 1), 0) < half
        low = jnp.sum(jnp.where(first, column, 0.0), axis=0, keepdims=True)
        high = jnp.sum(jnp.where(first, 0.0, column), axis=0, keepdims=True)
        return jnp.where(first, low, high) / width

    def to_columns(row):
        return jnp.broadcast_to(row, (128, chans)).T

    def transposes():
        gcol[...] = to_columns(gain[...])
        scol[...] = to_columns(shift[...])
        for i in range(chans // 128):
            span = slice(i * 128, (i + 1) * 128)
            xt[span, :] = lat[:, span].astype(F32).T

    def norm_forward():
        def body(i, carry):
            for u in range(UNROLL):
                span = pl.ds(pl.multiple_of((i * UNROLL + u) * block, block), block)
                values = xt[span, :]
                centered = values - group_mean(jnp.sum(values, axis=1, keepdims=True))
                spread = group_mean(jnp.sum(centered * centered, axis=1, keepdims=True))
                scale = lax.rsqrt(spread + 1e-5)
                normed = centered * scale
                pre = normed * gcol[span, :1] + scol[span, :1]
                nt[span, :] = normed
                rcol[span, :] = jnp.broadcast_to(scale, (block, 128))
                at[span, :] = pre / (1.0 + jnp.exp(-pre))
            return carry

        lax.fori_loop(0, blocks // UNROLL, body, 0)

    def make_patches():
        tall[krows:, :] = jnp.zeros((8, POS), F32)

        def taps(i, carry):
            start = pl.multiple_of(i * 80, 80)
            values = at[pl.ds(start, 80), :]
            for t, (down, right) in enumerate(TAPS):
                offset = 16 * down + right
                moved = values if offset == 0 else pltpu.roll(values, -offset % POS, 1)
                tall[pl.ds(t * chans + start, 80), :] = jnp.where(lane_mask(down, right), moved, 0.0)
            return carry

        lax.fori_loop(0, chans // 80, taps, 0)
        keep = lax.broadcasted_iota(jnp.int32, (SLAB, 1), 0) < shard

        def slabs(g, carry):
            for j in range(4):
                base, rest = j * shard // 8 * 8, j * shard % 8
                start = pl.multiple_of(g * (4 * shard) + base, 8)
                if rest:
                    values = pltpu.roll(tall[pl.ds(start, SLAB + 8), :], SLAB + 8 - rest, 0)[:SLAB]
                else:
                    values = tall[pl.ds(start, SLAB), :]
                pt[g * 4 + j] = jnp.where(keep, values, 0.0).astype(BF)
            return carry

        lax.fori_loop(0, count // 4, slabs, 0)

    def cotangent_shifts():
        for i in range(chans // 128):
            span = slice(i * 128, (i + 1) * 128)
            at[span, :] = cot[:, span].astype(F32).T

        def taps(i, carry):
            span = pl.ds(pl.multiple_of(i * 80, 80), 80)
            values = at[span, :]
            for t, (down, right) in enumerate(TAPS):
                offset = 16 * down + right
                moved = values if offset == 0 else pltpu.roll(values, offset % POS, 1)
                cs[t, span, :] = jnp.where(lane_mask(-down, -right), moved, 0.0).astype(BF)
            return carry

        lax.fori_loop(0, chans // 80, taps, 0)
        bacc[...] = jnp.zeros_like(bacc)

    def forward(first, last):
        def body(g, carry):
            group = pl.ds(g * 8, 8)
            acc[...] += lax.dot_general(
                pt[group].reshape(8 * SLAB, POS), wg[group].reshape(8 * SLAB, chans),
                (((0,), (0,)), ((), ())), preferred_element_type=F32,
            )
            return carry

        if first == 0:
            acc[...] = jnp.zeros_like(acc)
        lax.fori_loop(first, last, body, 0)
        if last == count // 8:
            out[...] = acc[...].astype(BF)

    def backward_tap(t):
        low = chans * t // shard
        slabs = (chans * t + chans - 1) // shard - low + 1
        grads = jnp.dot(
            wg[low : low + slabs].reshape(slabs * SLAB, chans), cs[t], preferred_element_type=F32
        )
        for j in range(slabs):
            first = shard * (low + j) - chans * t
            rest = first % 8
            start = SLAB + first - rest
            bacc[rest // 2, start : start + SLAB, :] += grads[j * SLAB : (j + 1) * SLAB]

    def backward_rest():
        lane = lax.broadcasted_iota(jnp.int32, (1, 128), 1)

        def one(i):
            start = pl.multiple_of(i * block, block)
            span = pl.ds(start, block)
            act_grad = bacc[0, pl.ds(start + SLAB, block), :]
            for r in (2, 4, 6):
                window = bacc[r // 2, pl.ds(start + SLAB - 8, block + 8), :]
                act_grad += pltpu.roll(window, block + r, 0)[:block]
            normed, gain_col = nt[span, :], gcol[span, :1]
            pre = normed * gain_col + scol[span, :1]
            sigma = 1.0 / (1.0 + jnp.exp(-pre))
            pre_grad = act_grad * sigma * (1.0 + pre * (1.0 - sigma))
            gain_grad = jnp.sum(pre_grad * normed, axis=1, keepdims=True)
            shift_grad = jnp.sum(pre_grad, axis=1, keepdims=True)
            ncol[span, :] = jnp.where(lane == 0, gain_grad, jnp.where(lane == 1, shift_grad, 0.0))
            first = group_mean(shift_grad * gain_col)
            second = group_mean(gain_grad * gain_col)
            xt[span, :] = rcol[span, :1] * (pre_grad * gain_col - first - normed * second)

        def body(i, carry):
            for u in range(UNROLL):
                one(i * UNROLL + u)
            return carry

        lax.fori_loop(0, blocks // UNROLL, body, 0)

    def write_input_grad():
        for i in range(chans // 128):
            span = slice(i * 128, (i + 1) * 128)
            in_grad[:, span] = xt[span, :].T.astype(BF)

    barrier = pltpu.get_barrier_semaphore()
    neighbours = [peer(d)[1] for peer in (peer1, peer2) for d in range(1, 8)] + list(partners)
    for device in neighbours:
        pl.semaphore_signal(barrier, inc=1, device_id=device, device_id_type=pl.DeviceIdType.MESH)
    wg[fs, SLAB - 16 :, :] = jnp.zeros((16, chans), BF)
    wg[fs, :shard, :] = w_in[...]
    transposes()
    pl.semaphore_wait(barrier, len(neighbours))

    ag_first()
    norm_forward()
    ag_near(z)
    make_patches()
    ag_far(z)
    ag_opposite()
    sibling_terms(0)
    own_terms(0)
    sibling_terms(1)
    rs_far(0)
    rs_near(0)
    ag_near(1 - z)
    ag_b(0)
    rs_far(1)
    rs_near(1)
    rs_late(0)
    own_terms(1)
    sibling_terms(2)
    ag_far(1 - z)
    ag_b(1)
    rs_far(2)
    rs_near(2)
    rs_late(1)
    ag_b(2)
    own_terms(2)
    sibling_terms(3)
    rs_far(3)
    rs_near(3)
    rs_late(2)
    rs_a_far(0)
    ag_b(3)
    ag_b_far(0)
    own_terms(3)
    rs_far(4)
    rs_near(4)
    rs_late(3)
    rs_a_near(0)
    ag_b(4)
    ag_b_far(1)
    cotangent_shifts()
    rs_far(5)
    rs_near(5)
    rs_late(4)
    rs_a_late(0)
    ag_b(5)
    ag_b_far(2)
    rs_far(6)
    rs_near(6)
    rs_late(5)
    ag_b(6)
    ag_b_far(3)
    rs_other_plane()
    rs_far(7)
    rs_near(7)
    rs_late(6)
    ag_b(7)
    ag_b_far(4)
    ag_b_far(5)
    rs_late(7)
    rs_a_far(1)
    ag_b_far(6)
    ag_b_far(7)
    rs_a_near(1)
    ag_sibling()
    for t in range(5):
        backward_tap(t)
    rs_a_late(1)
    for t in range(5, 9):
        backward_tap(t)
    rs_own_plane()
    backward_rest()
    norm_start(0, ncol[...].T[:8])
    write_input_grad()
    norm_start(1, norm_sum(0))
    forward(0, 4)
    norm_partner_start()
    forward(4, 8)
    rs_partner()
    norm_last()

    for copy in sent:
        copy.wait_send()
    for i in range(8):
        sib_copy(i).wait_send()
        b2_copy(i).wait_send()
        for way in range(2):
            b1_copy(i, way).wait_send()
    for h in range(2):
        a2_copy(h).wait_send()
        for way in range(2):
            a1_copy(h, way).wait_send()
    z_copy.wait_send()
    for copy in p_copies + n3_copies:
        copy.wait_send()
    for stage in range(2):
        for d in range(1, 8):
            norm_copy(stage, d, True).wait_send()


def shards(latents, cotangent, conv_weight, norm_gain, norm_shift, partner_bit):
    chans = latents.shape[3]
    shard = conv_weight.shape[1]
    count = lax.axis_size("fsdp")
    vmem = pl.BlockSpec(memory_space=pltpu.VMEM)
    piece = (SLAB, chans)
    dma = pltpu.SemaphoreType.DMA
    results = pl.pallas_call(
        kernel,
        out_shape=(
            jax.ShapeDtypeStruct((POS, chans), BF),
            jax.ShapeDtypeStruct((POS, chans), BF),
            jax.ShapeDtypeStruct((shard, 1, chans), F32),
            jax.ShapeDtypeStruct((2, chans), F32),
        ),
        in_specs=[vmem] * 5 + [pl.BlockSpec(memory_space=pltpu.SMEM)],
        out_specs=(vmem,) * 4,
        scratch_shapes=[
            pltpu.VMEM((count, *piece), BF),
            pltpu.VMEM((count, SLAB, POS), BF),
            pltpu.VMEM((count * shard + 8, POS), F32),
            pltpu.VMEM((9, chans, POS), BF),
            pltpu.VMEM((8, 4, *piece), F32),
            pltpu.VMEM((4, chans + 2 * SLAB, POS), F32),
            *[pltpu.VMEM((chans, POS), F32)] * 3,
            pltpu.VMEM((POS, chans), F32),
            *[pltpu.VMEM((chans, 128), F32)] * 4,
            pltpu.VMEM(piece, F32),
            *[pltpu.VMEM((8, 4, *piece), BF)] * 2,
            *[pltpu.VMEM((8, *piece), BF)] * 2,
            *[pltpu.VMEM((8, 2, *piece), BF)] * 2,
            *[pltpu.VMEM((2, *piece), BF)] * 2,
            *[pltpu.VMEM((2, 2, *piece), BF)] * 2,
            *[pltpu.VMEM(piece, BF)] * 2,
            pltpu.VMEM(piece, BF),
            pltpu.VMEM((2, *piece), BF),
            *[pltpu.VMEM((8, chans), F32), pltpu.VMEM((8, 8, chans), F32)] * 2,
            pltpu.VMEM((8, chans), F32),
            pltpu.VMEM((2, 8, chans), F32),
            dma((count,)), dma((count,)),
            dma((8,)), dma((8,)),
            dma((8,)), dma((8,)),
            dma((8, 2)), dma((8, 2)),
            dma((2,)), dma((2,)),
            dma((2, 2)), dma((2, 2)),
            dma, dma,
            dma((2,)), dma((2,)),
            dma((8,)), dma((8,)), dma((8,)), dma((8,)),
            dma((2,)), dma((2,)),
        ],
        compiler_params=pltpu.CompilerParams(
            collective_id=0, has_side_effects=True, vmem_limit_bytes=60 << 20
        ),
        name="block",
    )(
        latents.reshape(POS, chans), cotangent.reshape(POS, chans), conv_weight[0],
        norm_gain, norm_shift, partner_bit,
    )
    block_out, input_grad, weight_grad, norm_grad = results
    return (
        block_out.reshape(latents.shape),
        input_grad.reshape(latents.shape),
        weight_grad.reshape(1, shard, chans),
        norm_grad[None],
    )


def solution(mesh):
    in_specs = (
        P(("rep", "fsdp"), None, None, None),
        P(("rep", "fsdp"), None, None, None),
        P("rep", "fsdp", None),
        P("rep", None),
        P("rep", None),
        P(),
    )
    out_specs = (
        P(("rep", "fsdp"), None, None, None),
        P(("rep", "fsdp"), None, None, None),
        P("rep", "fsdp", None),
        P("rep", None, None),
    )
    return jax.shard_map(shards, mesh=mesh, in_specs=in_specs, out_specs=out_specs, check_vma=False)
```

```python
import jax
import jax.numpy as jnp
from jax import lax
from jax.experimental import pallas as pl
from jax.experimental.pallas import tpu as pltpu
from jax.sharding import PartitionSpec as P

GROUPS = 32
SIDE = 16
POS = SIDE * SIDE
SLAB = 96
UNROLL = 4
BF = jnp.bfloat16
F32 = jnp.float32
TAPS = [(a - 1, b - 1) for a in range(3) for b in range(3)]


def order(step):
    return (step + (step // 2) * (1 - 2 * (step % 2)) + 2) % 4


def lane_mask(down, right):
    lane = lax.broadcasted_iota(jnp.int32, (1, POS), 1)
    row, col = lane // SIDE + down, lane % SIDE + right
    return (row >= 0) & (row < SIDE) & (col >= 0) & (col < SIDE)


def kernel(
    lat, cot, w_in, gain, shift, bits, out, in_grad, w_grad, n_grad,
    wg, pt, tall, cs, tm, bacc, xt, nt, at, acc, gcol, scol, rcol, ncol, fin,
    sib_s, sib_r, b2_s, b2_r, b1_s, b1_r, a2_s, a2_r, a1_s, a1_r, z_s, z_r, p_s, p_r,
    n1_s, n1_r, n2_s, n2_r, n3_s, n3_r,
    ag_ss, ag_rs, sib_ss, sib_rs, b2_ss, b2_rs, b1_ss, b1_rs, a2_ss, a2_rs, a1_ss, a1_rs,
    z_ss, z_rs, p_ss, p_rs, n1_ss, n1_rs, n2_ss, n2_rs, n3_ss, n3_rs,
):
    chans = lat.shape[1]
    shard = w_in.shape[0]
    count = wg.shape[0]
    krows = count * shard
    rep, fs = lax.axis_index("rep"), lax.axis_index("fsdp")
    x, z, y, core = fs // 16, (fs // 8) % 2, (fs // 2) % 4, fs % 2
    a, b = x + (y - x) * core, y + (x - y) * core

    def slot(a_, z_, b_, core_):
        return (a_ % 4) * (16 - 14 * core_) + z_ * 8 + (b_ % 4) * (2 + 14 * core_) + core_

    def at_ab(da, db):
        return (rep, slot(a + da, z, b + db, core))

    sibling = (rep, fs + 1 - 2 * core)
    opposite = (rep, slot(a, 1 - z, b, core))
    partners = ((rep + 1 - 2 * (rep % 2), fs), (rep + 2 - 4 * (rep // 2), fs))

    def remote(src, dst, send_sem, recv_sem, device):
        return pltpu.make_async_remote_copy(
            src_ref=src, dst_ref=dst, send_sem=send_sem, recv_sem=recv_sem,
            device_id=device, device_id_type=pl.DeviceIdType.MESH,
        )

    sent = []

    def ag_send(index, *devices):
        for device in devices:
            copy = remote(wg.at[index], wg.at[index], ag_ss.at[len(sent)], ag_rs.at[index], device)
            copy.start()
            sent.append(copy)

    def ag_wait(index):
        remote(wg.at[index], wg.at[index], ag_ss.at[0], ag_rs.at[index], sibling).wait_recv()

    b_both = (at_ab(0, 1), at_ab(0, 3))
    a_both = (at_ab(1, 0), at_ab(3, 0))
    def of_plane(other):
        return 1 - z if other else z

    arrivals = [(0, 0), (3, 0), (1, 0), (0, 1), (2, 0), (3, 1), (1, 1), (2, 1)]

    def ag_first():
        ag_send(fs, opposite, *a_both, *b_both, sibling)

    def ag_near(other, side):
        zz, step = of_plane(other), 3 + 2 * (z + side)
        own = slot(a + step, zz, b, core)
        ag_wait(own)
        if other == side:
            ag_send(own, at_ab(1 + 2 * zz, 0))
        ag_send(own, *b_both, sibling)

    def ag_opposite():
        own = slot(a, 1 - z, b, core)
        ag_wait(own)
        ag_send(own, *a_both, *b_both, sibling)

    def ag_far(other):
        own = slot(a + 2, of_plane(other), b, core)
        ag_wait(own)
        ag_send(own, *b_both, sibling)

    def ag_b(k, side):
        da, other = arrivals[k]
        zz = of_plane(other)
        own = slot(a + da, zz, b + 3 + 2 * (z + side), core)
        ag_wait(own)
        if other == side:
            ag_send(own, at_ab(0, 1 + 2 * zz))
        ag_send(own, sibling)

    def ag_b_far(k):
        da, other = arrivals[k]
        own = slot(a + da, of_plane(other), b + 2, core)
        ag_wait(own)
        ag_send(own, sibling)

    def ag_sibling():
        def body(step, carry):
            ag_wait(2 * step + 1 - core)
            return carry

        lax.fori_loop(0, count // 2, body, 0)

    def plane(i):
        return z + (1 - 2 * z) * (1 - i // 4)

    def terms(first, indices):
        lhs = jnp.concatenate([pt[index] for index in indices], axis=0)
        return jnp.dot(lhs, cot[...], preferred_element_type=F32)

    def sib_copy(i):
        return remote(sib_s.at[i], sib_r.at[i], sib_ss.at[i], sib_rs.at[i], sibling)

    def sibling_terms(g):
        todo = [(i, jb) for i in (2 * g, 2 * g + 1) for jb in range(4)]
        value = terms(g, [slot(b + order(i % 4), plane(i), a + order(jb), 1 - core) for i, jb in todo])
        for n, (i, jb) in enumerate(todo):
            sib_s[i, jb] = value[n * SLAB : (n + 1) * SLAB].astype(BF)
            if jb == 3:
                sib_copy(i).start()

    def own_terms(g):
        todo = [(i, jb) for i in (2 * g, 2 * g + 1) for jb in range(4)]
        value = terms(g, [slot(a + order(i % 4), plane(i), b + order(jb), core) for i, jb in todo])
        for n, (i, jb) in enumerate(todo):
            tm[i, jb] = value[n * SLAB : (n + 1) * SLAB]

    def chip_term(i, jb):
        return tm[i, jb] + sib_r[i, jb].astype(F32)

    def b2_copy(i):
        return remote(b2_s.at[i], b2_r.at[i], b2_ss.at[i], b2_rs.at[i], at_ab(0, 1 + 2 * (i % 2)))

    def b1_copy(i, way):
        return remote(
            b1_s.at[i, way], b1_r.at[i, way], b1_ss.at[i, way], b1_rs.at[i, way],
            at_ab(0, 1 + 2 * way),
        )

    def rs_far(i):
        sib_copy(i).wait_recv()
        b2_s[i] = chip_term(i, 0).astype(BF)
        b2_copy(i).start()

    def rs_near(i):
        way = 1 - i % 2
        b1_s[i, way] = chip_term(i, 2 - way).astype(BF)
        b1_copy(i, way).start()

    def rs_late(i):
        way = i % 2
        b2_copy(i).wait_recv()
        b1_s[i, way] = (chip_term(i, 2 - way) + b2_r[i].astype(F32)).astype(BF)
        b1_copy(i, way).start()

    def row_term(i):
        for way in range(2):
            b1_copy(i, way).wait_recv()
        return chip_term(i, 3) + b1_r[i, 0].astype(F32) + b1_r[i, 1].astype(F32)

    def a2_copy(h):
        return remote(a2_s.at[h], a2_r.at[h], a2_ss.at[h], a2_rs.at[h], at_ab(1 + 2 * h, 0))

    def a1_copy(h, way):
        return remote(
            a1_s.at[h, way], a1_r.at[h, way], a1_ss.at[h, way], a1_rs.at[h, way],
            at_ab(1 + 2 * way, 0),
        )

    def rs_a_far(h):
        a2_s[h] = row_term(4 * h).astype(BF)
        a2_copy(h).start()

    def rs_a_near(h):
        way = 1 - h
        a1_s[h, way] = row_term(4 * h + 2 - way).astype(BF)
        a1_copy(h, way).start()

    def rs_a_late(h):
        way = h
        value = row_term(4 * h + 2 - way)
        a2_copy(h).wait_recv()
        a1_s[h, way] = (value + a2_r[h].astype(F32)).astype(BF)
        a1_copy(h, way).start()

    def plane_term(h):
        value = row_term(4 * h + 3)
        for way in range(2):
            a1_copy(h, way).wait_recv()
        return value + a1_r[h, 0].astype(F32) + a1_r[h, 1].astype(F32)

    z_copy = remote(z_s, z_r, z_ss, z_rs, opposite)
    p_copies = [remote(p_s, p_r.at[i], p_ss.at[i], p_rs.at[i], partners[i]) for i in range(2)]

    def rs_other_plane():
        z_s[...] = plane_term(0).astype(BF)
        z_copy.start()

    def rs_own_plane():
        value = plane_term(1)
        z_copy.wait_recv()
        value = value + z_r[...].astype(F32)
        fin[...] = value
        p_s[...] = value.astype(BF)
        for copy in p_copies:
            copy.start()

    def picked(index, first, second):
        second_share = bits[index].astype(F32)
        return first * (1.0 - second_share) + second * second_share

    def rs_partner():
        for copy in p_copies:
            copy.wait_recv()
        other = picked(fs, p_r[0].astype(F32), p_r[1].astype(F32))
        w_grad[...] = ((fin[...] + other) * (0.5 / count))[:shard].reshape(w_grad.shape)

    me1, me2 = x * 2 + core, z * 4 + y

    def peer1(d):
        other = (me1 + d) % 8
        return other, (rep, (other // 2) * 16 + z * 8 + y * 2 + other % 2)

    def peer2(d):
        other = (me2 + d) % 8
        return other, (rep, x * 16 + (other // 4) * 8 + (other % 4) * 2 + core)

    norm_stages = [(n1_s, n1_r, n1_ss, n1_rs, me1, peer1), (n2_s, n2_r, n2_ss, n2_rs, me2, peer2)]

    def norm_copy(stage, d, mine):
        send, recv, send_sems, recv_sems, me, peer = norm_stages[stage]
        other, device = peer(d)
        index = me if mine else other
        return remote(send, recv.at[index], send_sems.at[d], recv_sems.at[index], device)

    def norm_start(stage, value):
        send, recv, _, _, me, _ = norm_stages[stage]
        send[...] = value
        recv[me] = value
        for d in range(1, 8):
            norm_copy(stage, d, True).start()

    def norm_sum(stage):
        for d in range(1, 8):
            norm_copy(stage, d, False).wait_recv()
        recv = norm_stages[stage][1]
        total = recv[0]
        for i in range(1, 8):
            total = total + recv[i]
        return total

    n3_copies = [remote(n3_s, n3_r.at[i], n3_ss.at[i], n3_rs.at[i], partners[i]) for i in range(2)]

    def norm_partner_start():
        n3_s[...] = norm_sum(1)
        for copy in n3_copies:
            copy.start()

    def norm_last():
        for copy in n3_copies:
            copy.wait_recv()
        other = picked(0, n3_r[0], n3_r[1])
        n_grad[...] = ((n3_s[...] + other) * (0.5 / count))[:2]

    block = 40
    half = block // 2
    blocks = chans // block
    width = float(POS * (chans // GROUPS))

    def group_mean(column):
        first = lax.broadcasted_iota(jnp.int32, (block, 1), 0) < half
        low = jnp.sum(jnp.where(first, column, 0.0), axis=0, keepdims=True)
        high = jnp.sum(jnp.where(first, 0.0, column), axis=0, keepdims=True)
        return jnp.where(first, low, high) / width

    def to_columns(row):
        return jnp.broadcast_to(row, (128, chans)).T

    def transposes():
        gcol[...] = to_columns(gain[...])
        scol[...] = to_columns(shift[...])
        for i in range(chans // 128):
            span = slice(i * 128, (i + 1) * 128)
            xt[span, :] = lat[:, span].astype(F32).T

    def norm_forward():
        def body(i, carry):
            for u in range(UNROLL):
                span = pl.ds(pl.multiple_of((i * UNROLL + u) * block, block), block)
                values = xt[span, :]
                centered = values - group_mean(jnp.sum(values, axis=1, keepdims=True))
                spread = group_mean(jnp.sum(centered * centered, axis=1, keepdims=True))
                scale = lax.rsqrt(spread + 1e-5)
                normed = centered * scale
                pre = normed * gcol[span, :1] + scol[span, :1]
                nt[span, :] = normed
                rcol[span, :] = jnp.broadcast_to(scale, (block, 128))
                at[span, :] = pre / (1.0 + jnp.exp(-pre))
            return carry

        lax.fori_loop(0, blocks // UNROLL, body, 0)

    def make_patches():
        tall[krows:, :] = jnp.zeros((8, POS), F32)

        def taps(i, carry):
            start = pl.multiple_of(i * 80, 80)
            values = at[pl.ds(start, 80), :]
            for t, (down, right) in enumerate(TAPS):
                offset = 16 * down + right
                moved = values if offset == 0 else pltpu.roll(values, -offset % POS, 1)
                tall[pl.ds(t * chans + start, 80), :] = jnp.where(lane_mask(down, right), moved, 0.0)
            return carry

        lax.fori_loop(0, chans // 80, taps, 0)
        keep = lax.broadcasted_iota(jnp.int32, (SLAB, 1), 0) < shard

        def slabs(g, carry):
            for j in range(4):
                base, rest = j * shard // 8 * 8, j * shard % 8
                start = pl.multiple_of(g * (4 * shard) + base, 8)
                if rest:
                    values = pltpu.roll(tall[pl.ds(start, SLAB + 8), :], SLAB + 8 - rest, 0)[:SLAB]
                else:
                    values = tall[pl.ds(start, SLAB), :]
                pt[g * 4 + j] = jnp.where(keep, values, 0.0).astype(BF)
            return carry

        lax.fori_loop(0, count // 4, slabs, 0)

    def cotangent_shifts():
        for i in range(chans // 128):
            span = slice(i * 128, (i + 1) * 128)
            at[span, :] = cot[:, span].astype(F32).T

        def taps(i, carry):
            span = pl.ds(pl.multiple_of(i * 80, 80), 80)
            values = at[span, :]
            for t, (down, right) in enumerate(TAPS):
                offset = 16 * down + right
                moved = values if offset == 0 else pltpu.roll(values, offset % POS, 1)
                cs[t, span, :] = jnp.where(lane_mask(-down, -right), moved, 0.0).astype(BF)
            return carry

        lax.fori_loop(0, chans // 80, taps, 0)
        bacc[...] = jnp.zeros_like(bacc)

    def forward(first, last):
        def body(g, carry):
            group = pl.ds(g * 8, 8)
            acc[...] += lax.dot_general(
                pt[group].reshape(8 * SLAB, POS), wg[group].reshape(8 * SLAB, chans),
                (((0,), (0,)), ((), ())), preferred_element_type=F32,
            )
            return carry

        if first == 0:
            acc[...] = jnp.zeros_like(acc)
        lax.fori_loop(first, last, body, 0)
        if last == count // 8:
            out[...] = acc[...].astype(BF)

    def backward_tap(t):
        low = chans * t // shard
        slabs = (chans * t + chans - 1) // shard - low + 1
        grads = jnp.dot(
            wg[low : low + slabs].reshape(slabs * SLAB, chans), cs[t], preferred_element_type=F32
        )
        for j in range(slabs):
            first = shard * (low + j) - chans * t
            rest = first % 8
            start = SLAB + first - rest
            bacc[rest // 2, start : start + SLAB, :] += grads[j * SLAB : (j + 1) * SLAB]

    def backward_taps(first, last):
        for t in range(first, last):
            backward_tap(t)

    def backward_rest():
        lane = lax.broadcasted_iota(jnp.int32, (1, 128), 1)

        def one(i):
            start = pl.multiple_of(i * block, block)
            span = pl.ds(start, block)
            act_grad = bacc[0, pl.ds(start + SLAB, block), :]
            for r in (2, 4, 6):
                window = bacc[r // 2, pl.ds(start + SLAB - 8, block + 8), :]
                act_grad += pltpu.roll(window, block + r, 0)[:block]
            normed, gain_col = nt[span, :], gcol[span, :1]
            pre = normed * gain_col + scol[span, :1]
            sigma = 1.0 / (1.0 + jnp.exp(-pre))
            pre_grad = act_grad * sigma * (1.0 + pre * (1.0 - sigma))
            gain_grad = jnp.sum(pre_grad * normed, axis=1, keepdims=True)
            shift_grad = jnp.sum(pre_grad, axis=1, keepdims=True)
            ncol[span, :] = jnp.where(lane == 0, gain_grad, jnp.where(lane == 1, shift_grad, 0.0))
            first = group_mean(shift_grad * gain_col)
            second = group_mean(gain_grad * gain_col)
            xt[span, :] = rcol[span, :1] * (pre_grad * gain_col - first - normed * second)

        def body(i, carry):
            for u in range(UNROLL):
                one(i * UNROLL + u)
            return carry

        lax.fori_loop(0, blocks // UNROLL, body, 0)

    def write_input_grad():
        for i in range(chans // 128):
            span = slice(i * 128, (i + 1) * 128)
            in_grad[:, span] = xt[span, :].T.astype(BF)

    barrier = pltpu.get_barrier_semaphore()
    neighbours = [peer(d)[1] for peer in (peer1, peer2) for d in range(1, 8)] + list(partners)
    for device in neighbours:
        pl.semaphore_signal(barrier, inc=1, device_id=device, device_id_type=pl.DeviceIdType.MESH)
    wg[fs, SLAB - 16 :, :] = jnp.zeros((16, chans), BF)
    wg[fs, :shard, :] = w_in[...]
    transposes()
    pl.semaphore_wait(barrier, len(neighbours))

    ag_first()
    norm_forward()
    make_patches()
    ag_near(0, 0)
    ag_opposite()
    sibling_terms(0)
    own_terms(0)
    own_terms(3)
    own_terms(2)
    ag_near(0, 1)
    rs_far(0)
    sibling_terms(2)
    sibling_terms(1)
    rs_near(0)
    ag_far(0)
    ag_near(1, 1)
    sibling_terms(3)
    ag_b(3, 1)
    ag_b(2, 0)
    ag_near(1, 0)
    ag_b(0, 0)
    own_terms(1)
    cotangent_shifts()
    ag_far(1)
    ag_b(1, 0)
    ag_b(6, 1)
    rs_far(1)
    rs_far(2)
    ag_b(2, 1)
    ag_b(4, 0)
    rs_late(0)
    ag_b(5, 1)
    ag_b(7, 1)
    rs_far(3)
    ag_b(0, 1)
    ag_b(6, 0)
    rs_far(5)
    ag_b(3, 0)
    ag_b_far(6)
    ag_b_far(3)
    rs_far(4)
    rs_late(1)
    ag_b(1, 1)
    rs_near(2)
    ag_b_far(1)
    ag_b(4, 1)
    ag_b_far(2)
    rs_near(4)
    rs_near(1)
    ag_b_far(0)
    ag_b(5, 0)
    rs_far(7)
    ag_b(7, 0)
    rs_late(2)
    ag_b_far(5)
    ag_b_far(4)
    ag_b_far(7)
    rs_a_far(0)
    rs_late(3)
    ag_sibling()
    rs_late(4)
    rs_far(6)
    backward_taps(0, 3)
    rs_a_near(0)
    rs_near(3)
    rs_late(5)
    rs_near(5)
    backward_taps(3, 6)
    rs_near(6)
    rs_a_late(0)
    backward_taps(6, 9)
    rs_a_far(1)
    rs_late(6)
    backward_rest()
    rs_near(7)
    rs_late(7)
    rs_other_plane()
    norm_start(0, ncol[...].T[:8])
    rs_a_late(1)
    rs_a_near(1)
    forward(0, 2)
    norm_start(1, norm_sum(0))
    rs_own_plane()
    norm_partner_start()
    forward(2, 4)
    forward(4, 6)
    write_input_grad()
    forward(6, 8)
    rs_partner()
    norm_last()

    for copy in sent:
        copy.wait_send()
    for i in range(8):
        sib_copy(i).wait_send()
        b2_copy(i).wait_send()
        for way in range(2):
            b1_copy(i, way).wait_send()
    for h in range(2):
        a2_copy(h).wait_send()
        for way in range(2):
            a1_copy(h, way).wait_send()
    z_copy.wait_send()
    for copy in p_copies + n3_copies:
        copy.wait_send()
    for stage in range(2):
        for d in range(1, 8):
            norm_copy(stage, d, True).wait_send()


def finish(*refs):
    for source, target in zip(refs[: len(refs) // 2], refs[len(refs) // 2 :]):
        target[...] = source[...]


def shards(latents, cotangent, conv_weight, norm_gain, norm_shift, partner_bit):
    chans = latents.shape[3]
    shard = conv_weight.shape[1]
    count = lax.axis_size("fsdp")
    vmem = pl.BlockSpec(memory_space=pltpu.VMEM)
    piece = (SLAB, chans)
    dma = pltpu.SemaphoreType.DMA
    results = pl.pallas_call(
        kernel,
        out_shape=(
            jax.ShapeDtypeStruct((POS, chans), BF),
            jax.ShapeDtypeStruct((POS, chans), BF),
            jax.ShapeDtypeStruct((shard, 1, chans), F32),
            jax.ShapeDtypeStruct((2, chans), F32),
        ),
        in_specs=[vmem] * 5 + [pl.BlockSpec(memory_space=pltpu.SMEM)],
        out_specs=(vmem,) * 4,
        scratch_shapes=[
            pltpu.VMEM((count, *piece), BF),
            pltpu.VMEM((count, SLAB, POS), BF),
            pltpu.VMEM((count * shard + 8, POS), F32),
            pltpu.VMEM((9, chans, POS), BF),
            pltpu.VMEM((8, 4, *piece), F32),
            pltpu.VMEM((4, chans + 2 * SLAB, POS), F32),
            *[pltpu.VMEM((chans, POS), F32)] * 3,
            pltpu.VMEM((POS, chans), F32),
            *[pltpu.VMEM((chans, 128), F32)] * 4,
            pltpu.VMEM(piece, F32),
            *[pltpu.VMEM((8, 4, *piece), BF)] * 2,
            *[pltpu.VMEM((8, *piece), BF)] * 2,
            *[pltpu.VMEM((8, 2, *piece), BF)] * 2,
            *[pltpu.VMEM((2, *piece), BF)] * 2,
            *[pltpu.VMEM((2, 2, *piece), BF)] * 2,
            *[pltpu.VMEM(piece, BF)] * 2,
            pltpu.VMEM(piece, BF),
            pltpu.VMEM((2, *piece), BF),
            *[pltpu.VMEM((8, chans), F32), pltpu.VMEM((8, 8, chans), F32)] * 2,
            pltpu.VMEM((8, chans), F32),
            pltpu.VMEM((2, 8, chans), F32),
            dma((count,)), dma((count,)),
            dma((8,)), dma((8,)),
            dma((8,)), dma((8,)),
            dma((8, 2)), dma((8, 2)),
            dma((2,)), dma((2,)),
            dma((2, 2)), dma((2, 2)),
            dma, dma,
            dma((2,)), dma((2,)),
            dma((8,)), dma((8,)), dma((8,)), dma((8,)),
            dma((2,)), dma((2,)),
        ],
        compiler_params=pltpu.CompilerParams(
            collective_id=0, has_side_effects=True, vmem_limit_bytes=60 << 20
        ),
        name="block",
    )(
        latents.reshape(POS, chans), cotangent.reshape(POS, chans), conv_weight[0],
        norm_gain, norm_shift, partner_bit,
    )
    block_out, input_grad, weight_grad, norm_grad = pl.pallas_call(
        finish,
        out_shape=[jax.ShapeDtypeStruct(result.shape, result.dtype) for result in results],
        in_specs=[vmem] * 4,
        out_specs=[vmem] * 4,
        name="finish",
    )(*results)
    return (
        block_out.reshape(latents.shape),
        input_grad.reshape(latents.shape),
        weight_grad.reshape(1, shard, chans),
        norm_grad[None],
    )


def solution(mesh):
    in_specs = (
        P(("rep", "fsdp"), None, None, None),
        P(("rep", "fsdp"), None, None, None),
        P("rep", "fsdp", None),
        P("rep", None),
        P("rep", None),
        P(),
    )
    out_specs = (
        P(("rep", "fsdp"), None, None, None),
        P(("rep", "fsdp"), None, None, None),
        P("rep", "fsdp", None),
        P("rep", None, None),
    )
    return jax.shard_map(shards, mesh=mesh, in_specs=in_specs, out_specs=out_specs, check_vma=False)
```

```python
import jax
import jax.numpy as jnp
from jax import lax
from jax.experimental import pallas as pl
from jax.experimental.pallas import tpu as pltpu
from jax.sharding import PartitionSpec as P

GROUPS = 32
SIDE = 16
POS = SIDE * SIDE
SLAB = 96
UNROLL = 4
BF = jnp.bfloat16
F32 = jnp.float32
TAPS = [(a - 1, b - 1) for a in range(3) for b in range(3)]


def order(step):
    return (step + (step // 2) * (1 - 2 * (step % 2)) + 2) % 4


def lane_mask(down, right):
    lane = lax.broadcasted_iota(jnp.int32, (1, POS), 1)
    row, col = lane // SIDE + down, lane % SIDE + right
    return (row >= 0) & (row < SIDE) & (col >= 0) & (col < SIDE)


def kernel(
    lat_in, cot_in, w_in, gain, shift, bits, out, in_grad, w_grad, n_grad,
    lat, cot, w_own, wg, pt, tall, cs, tm, bacc, xt, nt, at, acc, gcol, scol, rcol, ncol, fin,
    sib_s, sib_r, b2_s, b2_r, b1_s, b1_r, a2_s, a2_r, a1_s, a1_r, z_s, z_r, p_s, p_r,
    n1_s, n1_r, n2_s, n2_r, n3_s, n3_r,
    ag_ss, ag_rs, sib_ss, sib_rs, b2_ss, b2_rs, b1_ss, b1_rs, a2_ss, a2_rs, a1_ss, a1_rs,
    z_ss, z_rs, p_ss, p_rs, n1_ss, n1_rs, n2_ss, n2_rs, n3_ss, n3_rs, in_s,
):
    chans = lat.shape[1]
    shard = w_in.shape[0]
    count = wg.shape[0]
    krows = count * shard
    rep, fs = lax.axis_index("rep"), lax.axis_index("fsdp")
    x, z, y, core = fs // 16, (fs // 8) % 2, (fs // 2) % 4, fs % 2
    a, b = x + (y - x) * core, y + (x - y) * core

    def slot(a_, z_, b_, core_):
        return (a_ % 4) * (16 - 14 * core_) + z_ * 8 + (b_ % 4) * (2 + 14 * core_) + core_

    def at_ab(da, db):
        return (rep, slot(a + da, z, b + db, core))

    sibling = (rep, fs + 1 - 2 * core)
    opposite = (rep, slot(a, 1 - z, b, core))
    partners = ((rep + 1 - 2 * (rep % 2), fs), (rep + 2 - 4 * (rep // 2), fs))

    def remote(src, dst, send_sem, recv_sem, device):
        return pltpu.make_async_remote_copy(
            src_ref=src, dst_ref=dst, send_sem=send_sem, recv_sem=recv_sem,
            device_id=device, device_id_type=pl.DeviceIdType.MESH,
        )

    sent = []

    def ag_send(index, *devices):
        for device in devices:
            copy = remote(wg.at[index], wg.at[index], ag_ss.at[len(sent)], ag_rs.at[index], device)
            copy.start()
            sent.append(copy)

    def ag_wait(index):
        remote(wg.at[index], wg.at[index], ag_ss.at[0], ag_rs.at[index], sibling).wait_recv()

    b_both = (at_ab(0, 1), at_ab(0, 3))
    a_both = (at_ab(1, 0), at_ab(3, 0))
    def of_plane(other):
        return 1 - z if other else z

    arrivals = [(0, 0), (3, 0), (1, 0), (0, 1), (2, 0), (3, 1), (1, 1), (2, 1)]

    def ag_first():
        ag_send(fs, opposite, *a_both, *b_both, sibling)

    def ag_near(other, side):
        zz, step = of_plane(other), 3 + 2 * (z + side)
        own = slot(a + step, zz, b, core)
        ag_wait(own)
        if other == side:
            ag_send(own, at_ab(1 + 2 * zz, 0))
        ag_send(own, *b_both, sibling)

    def ag_opposite():
        own = slot(a, 1 - z, b, core)
        ag_wait(own)
        ag_send(own, *a_both, *b_both, sibling)

    def ag_far(other):
        own = slot(a + 2, of_plane(other), b, core)
        ag_wait(own)
        ag_send(own, *b_both, sibling)

    def ag_b(k, side):
        da, other = arrivals[k]
        zz = of_plane(other)
        own = slot(a + da, zz, b + 3 + 2 * (z + side), core)
        ag_wait(own)
        if other == side:
            ag_send(own, at_ab(0, 1 + 2 * zz))
        ag_send(own, sibling)

    def ag_b_far(k):
        da, other = arrivals[k]
        own = slot(a + da, of_plane(other), b + 2, core)
        ag_wait(own)
        ag_send(own, sibling)

    def ag_sibling():
        def body(step, carry):
            ag_wait(2 * step + 1 - core)
            return carry

        lax.fori_loop(0, count // 2, body, 0)

    def plane(i):
        return z + (1 - 2 * z) * (1 - i // 4)

    def terms(first, indices):
        lhs = jnp.concatenate([pt[index] for index in indices], axis=0)
        return jnp.dot(lhs, cot[...], preferred_element_type=F32)

    def sib_copy(i):
        return remote(sib_s.at[i], sib_r.at[i], sib_ss.at[i], sib_rs.at[i], sibling)

    def sibling_terms(g):
        todo = [(i, jb) for i in (2 * g, 2 * g + 1) for jb in range(4)]
        value = terms(g, [slot(b + order(i % 4), plane(i), a + order(jb), 1 - core) for i, jb in todo])
        for n, (i, jb) in enumerate(todo):
            sib_s[i, jb] = value[n * SLAB : (n + 1) * SLAB].astype(BF)
            if jb == 3:
                sib_copy(i).start()

    def own_terms(g):
        todo = [(i, jb) for i in (2 * g, 2 * g + 1) for jb in range(4)]
        value = terms(g, [slot(a + order(i % 4), plane(i), b + order(jb), core) for i, jb in todo])
        for n, (i, jb) in enumerate(todo):
            tm[i, jb] = value[n * SLAB : (n + 1) * SLAB]

    def chip_term(i, jb):
        return tm[i, jb] + sib_r[i, jb].astype(F32)

    def b2_copy(i):
        return remote(b2_s.at[i], b2_r.at[i], b2_ss.at[i], b2_rs.at[i], at_ab(0, 1 + 2 * (i % 2)))

    def b1_copy(i, way):
        return remote(
            b1_s.at[i, way], b1_r.at[i, way], b1_ss.at[i, way], b1_rs.at[i, way],
            at_ab(0, 1 + 2 * way),
        )

    def rs_far(i):
        sib_copy(i).wait_recv()
        b2_s[i] = chip_term(i, 0).astype(BF)
        b2_copy(i).start()

    def rs_near(i):
        way = 1 - i % 2
        b1_s[i, way] = chip_term(i, 2 - way).astype(BF)
        b1_copy(i, way).start()

    def rs_late(i):
        way = i % 2
        b2_copy(i).wait_recv()
        b1_s[i, way] = (chip_term(i, 2 - way) + b2_r[i].astype(F32)).astype(BF)
        b1_copy(i, way).start()

    def row_term(i):
        for way in range(2):
            b1_copy(i, way).wait_recv()
        return chip_term(i, 3) + b1_r[i, 0].astype(F32) + b1_r[i, 1].astype(F32)

    def a2_copy(h):
        return remote(a2_s.at[h], a2_r.at[h], a2_ss.at[h], a2_rs.at[h], at_ab(1 + 2 * h, 0))

    def a1_copy(h, way):
        return remote(
            a1_s.at[h, way], a1_r.at[h, way], a1_ss.at[h, way], a1_rs.at[h, way],
            at_ab(1 + 2 * way, 0),
        )

    def rs_a_far(h):
        a2_s[h] = row_term(4 * h).astype(BF)
        a2_copy(h).start()

    def rs_a_near(h):
        way = 1 - h
        a1_s[h, way] = row_term(4 * h + 2 - way).astype(BF)
        a1_copy(h, way).start()

    def rs_a_late(h):
        way = h
        value = row_term(4 * h + 2 - way)
        a2_copy(h).wait_recv()
        a1_s[h, way] = (value + a2_r[h].astype(F32)).astype(BF)
        a1_copy(h, way).start()

    def plane_term(h):
        value = row_term(4 * h + 3)
        for way in range(2):
            a1_copy(h, way).wait_recv()
        return value + a1_r[h, 0].astype(F32) + a1_r[h, 1].astype(F32)

    z_copy = remote(z_s, z_r, z_ss, z_rs, opposite)
    p_copies = [remote(p_s, p_r.at[i], p_ss.at[i], p_rs.at[i], partners[i]) for i in range(2)]

    def rs_other_plane():
        z_s[...] = plane_term(0).astype(BF)
        z_copy.start()

    def rs_own_plane():
        value = plane_term(1)
        z_copy.wait_recv()
        value = value + z_r[...].astype(F32)
        fin[...] = value
        p_s[...] = value.astype(BF)
        for copy in p_copies:
            copy.start()

    def picked(index, first, second):
        second_share = bits[index].astype(F32)
        return first * (1.0 - second_share) + second * second_share

    def rs_partner():
        for copy in p_copies:
            copy.wait_recv()
        other = picked(fs, p_r[0].astype(F32), p_r[1].astype(F32))
        w_grad[...] = ((fin[...] + other) * (0.5 / count))[:shard].reshape(w_grad.shape)

    me1, me2 = x * 2 + core, z * 4 + y

    def peer1(d):
        other = (me1 + d) % 8
        return other, (rep, (other // 2) * 16 + z * 8 + y * 2 + other % 2)

    def peer2(d):
        other = (me2 + d) % 8
        return other, (rep, x * 16 + (other // 4) * 8 + (other % 4) * 2 + core)

    norm_stages = [(n1_s, n1_r, n1_ss, n1_rs, me1, peer1), (n2_s, n2_r, n2_ss, n2_rs, me2, peer2)]

    def norm_copy(stage, d, mine):
        send, recv, send_sems, recv_sems, me, peer = norm_stages[stage]
        other, device = peer(d)
        index = me if mine else other
        return remote(send, recv.at[index], send_sems.at[d], recv_sems.at[index], device)

    def norm_start(stage, value):
        send, recv, _, _, me, _ = norm_stages[stage]
        send[...] = value
        recv[me] = value
        for d in range(1, 8):
            norm_copy(stage, d, True).start()

    def norm_sum(stage):
        for d in range(1, 8):
            norm_copy(stage, d, False).wait_recv()
        recv = norm_stages[stage][1]
        total = recv[0]
        for i in range(1, 8):
            total = total + recv[i]
        return total

    n3_copies = [remote(n3_s, n3_r.at[i], n3_ss.at[i], n3_rs.at[i], partners[i]) for i in range(2)]

    def norm_partner_start():
        n3_s[...] = norm_sum(1)
        for copy in n3_copies:
            copy.start()

    def norm_last():
        for copy in n3_copies:
            copy.wait_recv()
        other = picked(0, n3_r[0], n3_r[1])
        n_grad[...] = ((n3_s[...] + other) * (0.5 / count))[:2]

    block = 40
    half = block // 2
    blocks = chans // block
    width = float(POS * (chans // GROUPS))

    def group_mean(column):
        first = lax.broadcasted_iota(jnp.int32, (block, 1), 0) < half
        low = jnp.sum(jnp.where(first, column, 0.0), axis=0, keepdims=True)
        high = jnp.sum(jnp.where(first, 0.0, column), axis=0, keepdims=True)
        return jnp.where(first, low, high) / width

    def to_columns(row):
        return jnp.broadcast_to(row, (128, chans)).T

    def transposes():
        gcol[...] = to_columns(gain[...])
        scol[...] = to_columns(shift[...])
        for i in range(chans // 128):
            span = slice(i * 128, (i + 1) * 128)
            xt[span, :] = lat[:, span].astype(F32).T

    def norm_forward():
        def body(i, carry):
            for u in range(UNROLL):
                span = pl.ds(pl.multiple_of((i * UNROLL + u) * block, block), block)
                values = xt[span, :]
                centered = values - group_mean(jnp.sum(values, axis=1, keepdims=True))
                spread = group_mean(jnp.sum(centered * centered, axis=1, keepdims=True))
                scale = lax.rsqrt(spread + 1e-5)
                normed = centered * scale
                pre = normed * gcol[span, :1] + scol[span, :1]
                nt[span, :] = normed
                rcol[span, :] = jnp.broadcast_to(scale, (block, 128))
                at[span, :] = pre / (1.0 + jnp.exp(-pre))
            return carry

        lax.fori_loop(0, blocks // UNROLL, body, 0)

    def make_patches():
        tall[krows:, :] = jnp.zeros((8, POS), F32)

        def taps(i, carry):
            start = pl.multiple_of(i * 80, 80)
            values = at[pl.ds(start, 80), :]
            for t, (down, right) in enumerate(TAPS):
                offset = 16 * down + right
                moved = values if offset == 0 else pltpu.roll(values, -offset % POS, 1)
                tall[pl.ds(t * chans + start, 80), :] = jnp.where(lane_mask(down, right), moved, 0.0)
            return carry

        lax.fori_loop(0, chans // 80, taps, 0)
        keep = lax.broadcasted_iota(jnp.int32, (SLAB, 1), 0) < shard

        def slabs(g, carry):
            for j in range(4):
                base, rest = j * shard // 8 * 8, j * shard % 8
                start = pl.multiple_of(g * (4 * shard) + base, 8)
                if rest:
                    values = pltpu.roll(tall[pl.ds(start, SLAB + 8), :], SLAB + 8 - rest, 0)[:SLAB]
                else:
                    values = tall[pl.ds(start, SLAB), :]
                pt[g * 4 + j] = jnp.where(keep, values, 0.0).astype(BF)
            return carry

        lax.fori_loop(0, count // 4, slabs, 0)

    def cotangent_shifts():
        for i in range(chans // 128):
            span = slice(i * 128, (i + 1) * 128)
            at[span, :] = cot[:, span].astype(F32).T

        def taps(i, carry):
            span = pl.ds(pl.multiple_of(i * 80, 80), 80)
            values = at[span, :]
            for t, (down, right) in enumerate(TAPS):
                offset = 16 * down + right
                moved = values if offset == 0 else pltpu.roll(values, offset % POS, 1)
                cs[t, span, :] = jnp.where(lane_mask(-down, -right), moved, 0.0).astype(BF)
            return carry

        lax.fori_loop(0, chans // 80, taps, 0)
        bacc[...] = jnp.zeros_like(bacc)

    def forward(first, last):
        def body(g, carry):
            group = pl.ds(g * 8, 8)
            acc[...] += lax.dot_general(
                pt[group].reshape(8 * SLAB, POS), wg[group].reshape(8 * SLAB, chans),
                (((0,), (0,)), ((), ())), preferred_element_type=F32,
            )
            return carry

        if first == 0:
            acc[...] = jnp.zeros_like(acc)
        lax.fori_loop(first, last, body, 0)
        if last == count // 8:
            out[...] = acc[...].astype(BF)

    def backward_tap(t):
        low = chans * t // shard
        slabs = (chans * t + chans - 1) // shard - low + 1
        grads = jnp.dot(
            wg[low : low + slabs].reshape(slabs * SLAB, chans), cs[t], preferred_element_type=F32
        )
        for j in range(slabs):
            first = shard * (low + j) - chans * t
            rest = first % 8
            start = SLAB + first - rest
            bacc[rest // 2, start : start + SLAB, :] += grads[j * SLAB : (j + 1) * SLAB]

    def backward_rest(part):
        lane = lax.broadcasted_iota(jnp.int32, (1, 128), 1)

        def one(i):
            start = pl.multiple_of(i * block, block)
            span = pl.ds(start, block)
            act_grad = bacc[0, pl.ds(start + SLAB, block), :]
            for r in (2, 4, 6):
                window = bacc[r // 2, pl.ds(start + SLAB - 8, block + 8), :]
                act_grad += pltpu.roll(window, block + r, 0)[:block]
            normed, gain_col = nt[span, :], gcol[span, :1]
            pre = normed * gain_col + scol[span, :1]
            sigma = 1.0 / (1.0 + jnp.exp(-pre))
            pre_grad = act_grad * sigma * (1.0 + pre * (1.0 - sigma))
            gain_grad = jnp.sum(pre_grad * normed, axis=1, keepdims=True)
            shift_grad = jnp.sum(pre_grad, axis=1, keepdims=True)
            ncol[span, :] = jnp.where(lane == 0, gain_grad, jnp.where(lane == 1, shift_grad, 0.0))
            first = group_mean(shift_grad * gain_col)
            second = group_mean(gain_grad * gain_col)
            xt[span, :] = rcol[span, :1] * (pre_grad * gain_col - first - normed * second)

        def body(i, carry):
            for u in range(UNROLL):
                one(i * UNROLL + u)
            return carry

        steps = blocks // UNROLL // 2
        lax.fori_loop(part * steps, (part + 1) * steps, body, 0)

    def write_input_grad():
        for i in range(chans // 128):
            span = slice(i * 128, (i + 1) * 128)
            in_grad[:, span] = xt[span, :].T.astype(BF)

    barrier = pltpu.get_barrier_semaphore()
    neighbours = [peer(d)[1] for peer in (peer1, peer2) for d in range(1, 8)] + list(partners)
    for device in neighbours:
        pl.semaphore_signal(barrier, inc=1, device_id=device, device_id_type=pl.DeviceIdType.MESH)
    arriving = [
        pltpu.make_async_copy(source, target, in_s.at[i])
        for i, (source, target) in enumerate(((w_in, w_own), (lat_in, lat), (cot_in, cot)))
    ]
    for copy in arriving:
        copy.start()
    wg[fs, SLAB - 16 :, :] = jnp.zeros((16, chans), BF)
    arriving[0].wait()
    wg[fs, :shard, :] = w_own[...]
    pl.semaphore_wait(barrier, len(neighbours))

    ag_first()
    arriving[1].wait()
    transposes()
    arriving[2].wait()
    norm_forward()
    make_patches()
    ag_near(0, 0)
    sibling_terms(0)
    own_terms(0)
    ag_opposite()
    sibling_terms(1)
    rs_far(1)
    rs_far(0)
    ag_near(0, 1)
    ag_far(0)
    own_terms(1)
    rs_far(2)
    sibling_terms(2)
    ag_near(1, 1)
    ag_b(0, 0)
    ag_near(1, 0)
    ag_b(0, 1)
    ag_b(3, 1)
    rs_near(0)
    ag_b(1, 0)
    ag_b(1, 1)
    own_terms(2)
    rs_late(0)
    ag_b(2, 0)
    cotangent_shifts()
    rs_far(4)
    ag_b(4, 0)
    ag_far(1)
    ag_b(3, 0)
    ag_b(6, 1)
    ag_b(5, 1)
    ag_b(2, 1)
    ag_b_far(0)
    rs_far(3)
    ag_b(7, 1)
    sibling_terms(3)
    rs_near(1)
    rs_late(1)
    ag_b(5, 0)
    ag_b_far(6)
    own_terms(3)
    rs_near(2)
    rs_late(2)
    ag_b(6, 0)
    ag_b_far(5)
    ag_b_far(3)
    ag_b_far(2)
    ag_b_far(1)
    rs_far(5)
    rs_a_far(0)
    rs_late(4)
    rs_near(4)
    rs_far(7)
    rs_far(6)
    rs_near(3)
    ag_b_far(4)
    ag_b_far(7)
    rs_late(3)
    rs_near(5)
    rs_near(6)
    ag_b(7, 0)
    ag_b(4, 1)
    ag_sibling()
    backward_tap(5)
    rs_a_near(0)
    backward_tap(0)
    backward_tap(7)
    backward_tap(2)
    backward_tap(3)
    backward_tap(1)
    rs_a_late(0)
    backward_tap(6)
    backward_tap(4)
    backward_tap(8)
    rs_late(5)
    backward_rest(1)
    rs_a_far(1)
    rs_late(6)
    backward_rest(0)
    norm_start(0, ncol[...].T[:8])
    rs_other_plane()
    rs_near(7)
    rs_late(7)
    rs_a_near(1)
    rs_a_late(1)
    forward(0, 2)
    norm_start(1, norm_sum(0))
    forward(2, 4)
    write_input_grad()
    rs_own_plane()
    forward(4, 6)
    forward(6, 8)
    norm_partner_start()
    rs_partner()
    norm_last()

    for copy in sent:
        copy.wait_send()
    for i in range(8):
        sib_copy(i).wait_send()
        b2_copy(i).wait_send()
        for way in range(2):
            b1_copy(i, way).wait_send()
    for h in range(2):
        a2_copy(h).wait_send()
        for way in range(2):
            a1_copy(h, way).wait_send()
    z_copy.wait_send()
    for copy in p_copies + n3_copies:
        copy.wait_send()
    for stage in range(2):
        for d in range(1, 8):
            norm_copy(stage, d, True).wait_send()


def finish(*refs):
    for source, target in zip(refs[: len(refs) // 2], refs[len(refs) // 2 :]):
        target[...] = source[...]


def shards(latents, cotangent, conv_weight, norm_gain, norm_shift, partner_bit):
    chans = latents.shape[3]
    shard = conv_weight.shape[1]
    count = lax.axis_size("fsdp")
    vmem = pl.BlockSpec(memory_space=pltpu.VMEM)
    anywhere = pl.BlockSpec(memory_space=pl.ANY)
    piece = (SLAB, chans)
    dma = pltpu.SemaphoreType.DMA
    results = pl.pallas_call(
        kernel,
        out_shape=(
            jax.ShapeDtypeStruct((POS, chans), BF),
            jax.ShapeDtypeStruct((POS, chans), BF),
            jax.ShapeDtypeStruct((shard, 1, chans), F32),
            jax.ShapeDtypeStruct((2, chans), F32),
        ),
        in_specs=[anywhere] * 3 + [vmem] * 2 + [pl.BlockSpec(memory_space=pltpu.SMEM)],
        out_specs=(vmem,) * 4,
        scratch_shapes=[
            pltpu.VMEM((POS, chans), BF),
            pltpu.VMEM((POS, chans), BF),
            pltpu.VMEM((shard, chans), BF),
            pltpu.VMEM((count, *piece), BF),
            pltpu.VMEM((count, SLAB, POS), BF),
            pltpu.VMEM((count * shard + 8, POS), F32),
            pltpu.VMEM((9, chans, POS), BF),
            pltpu.VMEM((8, 4, *piece), F32),
            pltpu.VMEM((4, chans + 2 * SLAB, POS), F32),
            *[pltpu.VMEM((chans, POS), F32)] * 3,
            pltpu.VMEM((POS, chans), F32),
            *[pltpu.VMEM((chans, 128), F32)] * 4,
            pltpu.VMEM(piece, F32),
            *[pltpu.VMEM((8, 4, *piece), BF)] * 2,
            *[pltpu.VMEM((8, *piece), BF)] * 2,
            *[pltpu.VMEM((8, 2, *piece), BF)] * 2,
            *[pltpu.VMEM((2, *piece), BF)] * 2,
            *[pltpu.VMEM((2, 2, *piece), BF)] * 2,
            *[pltpu.VMEM(piece, BF)] * 2,
            pltpu.VMEM(piece, BF),
            pltpu.VMEM((2, *piece), BF),
            *[pltpu.VMEM((8, chans), F32), pltpu.VMEM((8, 8, chans), F32)] * 2,
            pltpu.VMEM((8, chans), F32),
            pltpu.VMEM((2, 8, chans), F32),
            dma((count,)), dma((count,)),
            dma((8,)), dma((8,)),
            dma((8,)), dma((8,)),
            dma((8, 2)), dma((8, 2)),
            dma((2,)), dma((2,)),
            dma((2, 2)), dma((2, 2)),
            dma, dma,
            dma((2,)), dma((2,)),
            dma((8,)), dma((8,)), dma((8,)), dma((8,)),
            dma((2,)), dma((2,)), dma((3,)),
        ],
        compiler_params=pltpu.CompilerParams(
            collective_id=0, has_side_effects=True, vmem_limit_bytes=60 << 20
        ),
        name="block",
    )(
        latents.reshape(POS, chans), cotangent.reshape(POS, chans), conv_weight[0],
        norm_gain, norm_shift, partner_bit,
    )
    block_out, input_grad, weight_grad, norm_grad = pl.pallas_call(
        finish,
        out_shape=[jax.ShapeDtypeStruct(result.shape, result.dtype) for result in results],
        in_specs=[vmem] * 4,
        out_specs=[vmem] * 4,
        name="finish",
    )(*results)
    return (
        block_out.reshape(latents.shape),
        input_grad.reshape(latents.shape),
        weight_grad.reshape(1, shard, chans),
        norm_grad[None],
    )


def solution(mesh):
    in_specs = (
        P(("rep", "fsdp"), None, None, None),
        P(("rep", "fsdp"), None, None, None),
        P("rep", "fsdp", None),
        P("rep", None),
        P("rep", None),
        P(),
    )
    out_specs = (
        P(("rep", "fsdp"), None, None, None),
        P(("rep", "fsdp"), None, None, None),
        P("rep", "fsdp", None),
        P("rep", None, None),
    )
    return jax.shard_map(shards, mesh=mesh, in_specs=in_specs, out_specs=out_specs, check_vma=False)
```

```python
import jax
import jax.numpy as jnp
from jax import lax
from jax.experimental import pallas as pl
from jax.experimental.pallas import tpu as pltpu
from jax.sharding import PartitionSpec as P

GROUPS = 32
SIDE = 16
POS = SIDE * SIDE
SLAB = 96
UNROLL = 4
BF = jnp.bfloat16
F32 = jnp.float32
TAPS = [(a - 1, b - 1) for a in range(3) for b in range(3)]


def order(step):
    return (step + (step // 2) * (1 - 2 * (step % 2)) + 2) % 4


def lane_mask(down, right):
    lane = lax.broadcasted_iota(jnp.int32, (1, POS), 1)
    row, col = lane // SIDE + down, lane % SIDE + right
    return (row >= 0) & (row < SIDE) & (col >= 0) & (col < SIDE)


def kernel(
    lat_in, cot_in, w_in, gain, shift, bits, out, in_grad, w_grad, n_grad,
    lat, cot, w_own, wg, pt, tall, cs, tm, bacc, xt, nt, at, acc, gcol, scol, rcol, ncol, fin,
    sib_s, sib_r, b2_s, b2_r, b1_s, b1_r, a2_s, a2_r, a1_s, a1_r, z_s, z_r, p_s, p_r,
    n1_s, n1_r, n2_s, n2_r, n3_s, n3_r,
    ag_ss, ag_rs, sib_ss, sib_rs, b2_ss, b2_rs, b1_ss, b1_rs, a2_ss, a2_rs, a1_ss, a1_rs,
    z_ss, z_rs, p_ss, p_rs, n1_ss, n1_rs, n2_ss, n2_rs, n3_ss, n3_rs, in_s,
):
    chans = lat.shape[1]
    shard = w_in.shape[0]
    count = wg.shape[0]
    krows = count * shard
    rep, fs = lax.axis_index("rep"), lax.axis_index("fsdp")
    x, z, y, core = fs // 16, (fs // 8) % 2, (fs // 2) % 4, fs % 2
    a, b = x + (y - x) * core, y + (x - y) * core

    def slot(a_, z_, b_, core_):
        return (a_ % 4) * (16 - 14 * core_) + z_ * 8 + (b_ % 4) * (2 + 14 * core_) + core_

    def at_ab(da, db):
        return (rep, slot(a + da, z, b + db, core))

    sibling = (rep, fs + 1 - 2 * core)
    opposite = (rep, slot(a, 1 - z, b, core))
    partners = ((rep + 1 - 2 * (rep % 2), fs), (rep + 2 - 4 * (rep // 2), fs))

    def remote(src, dst, send_sem, recv_sem, device):
        return pltpu.make_async_remote_copy(
            src_ref=src, dst_ref=dst, send_sem=send_sem, recv_sem=recv_sem,
            device_id=device, device_id_type=pl.DeviceIdType.MESH,
        )

    sent = []

    def ag_send(index, *devices):
        for device in devices:
            copy = remote(wg.at[index], wg.at[index], ag_ss.at[len(sent)], ag_rs.at[index], device)
            copy.start()
            sent.append(copy)

    def ag_wait(index):
        remote(wg.at[index], wg.at[index], ag_ss.at[0], ag_rs.at[index], sibling).wait_recv()

    b_both = (at_ab(0, 1), at_ab(0, 3))
    a_both = (at_ab(1, 0), at_ab(3, 0))
    def of_plane(other):
        return 1 - z if other else z

    arrivals = [(0, 0), (3, 0), (1, 0), (0, 1), (2, 0), (3, 1), (1, 1), (2, 1)]

    def ag_first():
        ag_send(fs, opposite, *a_both, *b_both, sibling)

    def ag_near(other, side):
        zz, step = of_plane(other), 3 + 2 * (z + side)
        own = slot(a + step, zz, b, core)
        ag_wait(own)
        if other == side:
            ag_send(own, at_ab(1 + 2 * zz, 0))
        ag_send(own, *b_both, sibling)

    def ag_opposite():
        own = slot(a, 1 - z, b, core)
        ag_wait(own)
        ag_send(own, *a_both, *b_both, sibling)

    def ag_far(other):
        own = slot(a + 2, of_plane(other), b, core)
        ag_wait(own)
        ag_send(own, *b_both, sibling)

    def ag_b(k, side):
        da, other = arrivals[k]
        zz = of_plane(other)
        own = slot(a + da, zz, b + 3 + 2 * (z + side), core)
        ag_wait(own)
        if other == side:
            ag_send(own, at_ab(0, 1 + 2 * zz))
        ag_send(own, sibling)

    def ag_b_far(k):
        da, other = arrivals[k]
        own = slot(a + da, of_plane(other), b + 2, core)
        ag_wait(own)
        ag_send(own, sibling)

    def ag_sibling():
        def body(step, carry):
            ag_wait(2 * step + 1 - core)
            return carry

        lax.fori_loop(0, count // 2, body, 0)

    def plane(i):
        return z + (1 - 2 * z) * (1 - i // 4)

    def terms(first, indices):
        lhs = jnp.concatenate([pt[index] for index in indices], axis=0)
        return jnp.dot(lhs, cot[...], preferred_element_type=F32)

    def sib_copy(i):
        return remote(sib_s.at[i], sib_r.at[i], sib_ss.at[i], sib_rs.at[i], sibling)

    def sibling_terms(g):
        todo = [(i, jb) for i in (2 * g, 2 * g + 1) for jb in range(4)]
        value = terms(g, [slot(b + order(i % 4), plane(i), a + order(jb), 1 - core) for i, jb in todo])
        for n, (i, jb) in enumerate(todo):
            sib_s[i, jb] = value[n * SLAB : (n + 1) * SLAB].astype(BF)
            if jb == 3:
                sib_copy(i).start()

    def own_terms(g):
        todo = [(i, jb) for i in (2 * g, 2 * g + 1) for jb in range(4)]
        value = terms(g, [slot(a + order(i % 4), plane(i), b + order(jb), core) for i, jb in todo])
        for n, (i, jb) in enumerate(todo):
            tm[i, jb] = value[n * SLAB : (n + 1) * SLAB]

    def chip_term(i, jb):
        return tm[i, jb] + sib_r[i, jb].astype(F32)

    def b2_copy(i):
        return remote(b2_s.at[i], b2_r.at[i], b2_ss.at[i], b2_rs.at[i], at_ab(0, 1 + 2 * (i % 2)))

    def b1_copy(i, way):
        return remote(
            b1_s.at[i, way], b1_r.at[i, way], b1_ss.at[i, way], b1_rs.at[i, way],
            at_ab(0, 1 + 2 * way),
        )

    def rs_far(i):
        sib_copy(i).wait_recv()
        b2_s[i] = chip_term(i, 0).astype(BF)
        b2_copy(i).start()

    def rs_near(i):
        way = 1 - i % 2
        b1_s[i, way] = chip_term(i, 2 - way).astype(BF)
        b1_copy(i, way).start()

    def rs_late(i):
        way = i % 2
        b2_copy(i).wait_recv()
        b1_s[i, way] = (chip_term(i, 2 - way) + b2_r[i].astype(F32)).astype(BF)
        b1_copy(i, way).start()

    def row_term(i):
        for way in range(2):
            b1_copy(i, way).wait_recv()
        return chip_term(i, 3) + b1_r[i, 0].astype(F32) + b1_r[i, 1].astype(F32)

    def a2_copy(h):
        return remote(a2_s.at[h], a2_r.at[h], a2_ss.at[h], a2_rs.at[h], at_ab(1 + 2 * h, 0))

    def a1_copy(h, way):
        return remote(
            a1_s.at[h, way], a1_r.at[h, way], a1_ss.at[h, way], a1_rs.at[h, way],
            at_ab(1 + 2 * way, 0),
        )

    def rs_a_far(h):
        a2_s[h] = row_term(4 * h).astype(BF)
        a2_copy(h).start()

    def rs_a_near(h):
        way = 1 - h
        a1_s[h, way] = row_term(4 * h + 2 - way).astype(BF)
        a1_copy(h, way).start()

    def rs_a_late(h):
        way = h
        value = row_term(4 * h + 2 - way)
        a2_copy(h).wait_recv()
        a1_s[h, way] = (value + a2_r[h].astype(F32)).astype(BF)
        a1_copy(h, way).start()

    def plane_term(h):
        value = row_term(4 * h + 3)
        for way in range(2):
            a1_copy(h, way).wait_recv()
        return value + a1_r[h, 0].astype(F32) + a1_r[h, 1].astype(F32)

    z_copy = remote(z_s, z_r, z_ss, z_rs, opposite)
    p_copies = [remote(p_s, p_r.at[i], p_ss.at[i], p_rs.at[i], partners[i]) for i in range(2)]

    def rs_other_plane():
        z_s[...] = plane_term(0).astype(BF)
        z_copy.start()

    def rs_own_plane():
        value = plane_term(1)
        z_copy.wait_recv()
        value = value + z_r[...].astype(F32)
        fin[...] = value
        p_s[...] = value.astype(BF)
        for copy in p_copies:
            copy.start()

    def picked(index, first, second):
        second_share = bits[index].astype(F32)
        return first * (1.0 - second_share) + second * second_share

    def rs_partner():
        for copy in p_copies:
            copy.wait_recv()
        other = picked(fs, p_r[0].astype(F32), p_r[1].astype(F32))
        w_grad[...] = ((fin[...] + other) * (0.5 / count))[:shard].reshape(w_grad.shape)

    me1, me2 = x * 2 + core, z * 4 + y

    def peer1(d):
        other = (me1 + d) % 8
        return other, (rep, (other // 2) * 16 + z * 8 + y * 2 + other % 2)

    def peer2(d):
        other = (me2 + d) % 8
        return other, (rep, x * 16 + (other // 4) * 8 + (other % 4) * 2 + core)

    norm_stages = [(n1_s, n1_r, n1_ss, n1_rs, me1, peer1), (n2_s, n2_r, n2_ss, n2_rs, me2, peer2)]

    def norm_copy(stage, d, mine):
        send, recv, send_sems, recv_sems, me, peer = norm_stages[stage]
        other, device = peer(d)
        index = me if mine else other
        return remote(send, recv.at[index], send_sems.at[d], recv_sems.at[index], device)

    def norm_start(stage, value):
        send, recv, _, _, me, _ = norm_stages[stage]
        send[...] = value
        recv[me] = value
        for d in range(1, 8):
            norm_copy(stage, d, True).start()

    def norm_sum(stage):
        for d in range(1, 8):
            norm_copy(stage, d, False).wait_recv()
        recv = norm_stages[stage][1]
        total = recv[0]
        for i in range(1, 8):
            total = total + recv[i]
        return total

    n3_copies = [remote(n3_s, n3_r.at[i], n3_ss.at[i], n3_rs.at[i], partners[i]) for i in range(2)]

    def norm_partner_start():
        n3_s[...] = norm_sum(1)
        for copy in n3_copies:
            copy.start()

    def norm_last():
        for copy in n3_copies:
            copy.wait_recv()
        other = picked(0, n3_r[0], n3_r[1])
        n_grad[...] = ((n3_s[...] + other) * (0.5 / count))[:2]

    block = 40
    half = block // 2
    blocks = chans // block
    width = float(POS * (chans // GROUPS))

    def group_mean(column):
        first = lax.broadcasted_iota(jnp.int32, (block, 1), 0) < half
        low = jnp.sum(jnp.where(first, column, 0.0), axis=0, keepdims=True)
        high = jnp.sum(jnp.where(first, 0.0, column), axis=0, keepdims=True)
        return jnp.where(first, low, high) / width

    def to_columns(row):
        return jnp.broadcast_to(row, (128, chans)).T

    def transposes():
        gcol[...] = to_columns(gain[...])
        scol[...] = to_columns(shift[...])
        for i in range(chans // 128):
            span = slice(i * 128, (i + 1) * 128)
            xt[span, :] = lat[:, span].astype(F32).T

    def norm_forward():
        def body(i, carry):
            for u in range(UNROLL):
                span = pl.ds(pl.multiple_of((i * UNROLL + u) * block, block), block)
                values = xt[span, :]
                centered = values - group_mean(jnp.sum(values, axis=1, keepdims=True))
                spread = group_mean(jnp.sum(centered * centered, axis=1, keepdims=True))
                scale = lax.rsqrt(spread + 1e-5)
                normed = centered * scale
                pre = normed * gcol[span, :1] + scol[span, :1]
                nt[span, :] = normed
                rcol[span, :] = jnp.broadcast_to(scale, (block, 128))
                at[span, :] = pre / (1.0 + jnp.exp(-pre))
            return carry

        lax.fori_loop(0, blocks // UNROLL, body, 0)

    def make_patches():
        tall[krows:, :] = jnp.zeros((8, POS), F32)

        def taps(i, carry):
            start = pl.multiple_of(i * 80, 80)
            values = at[pl.ds(start, 80), :]
            for t, (down, right) in enumerate(TAPS):
                offset = 16 * down + right
                moved = values if offset == 0 else pltpu.roll(values, -offset % POS, 1)
                tall[pl.ds(t * chans + start, 80), :] = jnp.where(lane_mask(down, right), moved, 0.0)
            return carry

        lax.fori_loop(0, chans // 80, taps, 0)
        keep = lax.broadcasted_iota(jnp.int32, (SLAB, 1), 0) < shard

        def slabs(g, carry):
            for j in range(4):
                base, rest = j * shard // 8 * 8, j * shard % 8
                start = pl.multiple_of(g * (4 * shard) + base, 8)
                if rest:
                    values = pltpu.roll(tall[pl.ds(start, SLAB + 8), :], SLAB + 8 - rest, 0)[:SLAB]
                else:
                    values = tall[pl.ds(start, SLAB), :]
                pt[g * 4 + j] = jnp.where(keep, values, 0.0).astype(BF)
            return carry

        lax.fori_loop(0, count // 4, slabs, 0)

    def cotangent_shifts():
        for i in range(chans // 128):
            span = slice(i * 128, (i + 1) * 128)
            at[span, :] = cot[:, span].astype(F32).T

        def taps(i, carry):
            span = pl.ds(pl.multiple_of(i * 80, 80), 80)
            values = at[span, :]
            for t, (down, right) in enumerate(TAPS):
                offset = 16 * down + right
                moved = values if offset == 0 else pltpu.roll(values, offset % POS, 1)
                cs[t, span, :] = jnp.where(lane_mask(-down, -right), moved, 0.0).astype(BF)
            return carry

        lax.fori_loop(0, chans // 80, taps, 0)
        bacc[...] = jnp.zeros_like(bacc)

    def forward(first, last):
        def body(g, carry):
            group = pl.ds(g * 8, 8)
            acc[...] += lax.dot_general(
                pt[group].reshape(8 * SLAB, POS), wg[group].reshape(8 * SLAB, chans),
                (((0,), (0,)), ((), ())), preferred_element_type=F32,
            )
            return carry

        if first == 0:
            acc[...] = jnp.zeros_like(acc)
        lax.fori_loop(first, last, body, 0)
        if last == count // 8:
            out[...] = acc[...].astype(BF)

    def backward_tap(t):
        low = chans * t // shard
        slabs = (chans * t + chans - 1) // shard - low + 1
        grads = jnp.dot(
            wg[low : low + slabs].reshape(slabs * SLAB, chans), cs[t], preferred_element_type=F32
        )
        for j in range(slabs):
            first = shard * (low + j) - chans * t
            rest = first % 8
            start = SLAB + first - rest
            bacc[rest // 2, start : start + SLAB, :] += grads[j * SLAB : (j + 1) * SLAB]

    def backward_rest(part):
        lane = lax.broadcasted_iota(jnp.int32, (1, 128), 1)

        def one(i):
            start = pl.multiple_of(i * block, block)
            span = pl.ds(start, block)
            act_grad = bacc[0, pl.ds(start + SLAB, block), :]
            for r in (2, 4, 6):
                window = bacc[r // 2, pl.ds(start + SLAB - 8, block + 8), :]
                act_grad += pltpu.roll(window, block + r, 0)[:block]
            normed, gain_col = nt[span, :], gcol[span, :1]
            pre = normed * gain_col + scol[span, :1]
            sigma = 1.0 / (1.0 + jnp.exp(-pre))
            pre_grad = act_grad * sigma * (1.0 + pre * (1.0 - sigma))
            gain_grad = jnp.sum(pre_grad * normed, axis=1, keepdims=True)
            shift_grad = jnp.sum(pre_grad, axis=1, keepdims=True)
            ncol[span, :] = jnp.where(lane == 0, gain_grad, jnp.where(lane == 1, shift_grad, 0.0))
            first = group_mean(shift_grad * gain_col)
            second = group_mean(gain_grad * gain_col)
            xt[span, :] = rcol[span, :1] * (pre_grad * gain_col - first - normed * second)

        def body(i, carry):
            for u in range(UNROLL):
                one(i * UNROLL + u)
            return carry

        steps = blocks // UNROLL // 2
        lax.fori_loop(part * steps, (part + 1) * steps, body, 0)

    def write_input_grad():
        for i in range(chans // 128):
            span = slice(i * 128, (i + 1) * 128)
            in_grad[:, span] = xt[span, :].T.astype(BF)

    barrier = pltpu.get_barrier_semaphore()
    neighbours = [peer(d)[1] for peer in (peer1, peer2) for d in range(1, 8)] + list(partners)
    for device in neighbours:
        pl.semaphore_signal(barrier, inc=1, device_id=device, device_id_type=pl.DeviceIdType.MESH)
    arriving = [
        pltpu.make_async_copy(source, target, in_s.at[i])
        for i, (source, target) in enumerate(((w_in, w_own), (lat_in, lat), (cot_in, cot)))
    ]
    for copy in arriving:
        copy.start()
    wg[fs, SLAB - 16 :, :] = jnp.zeros((16, chans), BF)
    arriving[0].wait()
    wg[fs, :shard, :] = w_own[...]
    pl.semaphore_wait(barrier, len(neighbours))

    ag_first()
    arriving[1].wait()
    transposes()
    arriving[2].wait()
    norm_forward()
    make_patches()
    ag_near(0, 0)
    ag_opposite()
    sibling_terms(0)
    own_terms(0)
    own_terms(2)
    ag_near(0, 1)
    own_terms(1)
    rs_far(0)
    rs_near(0)
    cotangent_shifts()
    ag_far(0)
    ag_near(1, 1)
    sibling_terms(1)
    own_terms(3)
    ag_b(2, 1)
    ag_near(1, 0)
    rs_far(2)
    rs_far(1)
    sibling_terms(2)
    ag_b(1, 0)
    rs_late(0)
    ag_b(2, 0)
    ag_b(0, 0)
    ag_b(3, 1)
    rs_far(4)
    ag_b(4, 0)
    ag_far(1)
    ag_b(6, 1)
    ag_b(5, 1)
    rs_far(3)
    ag_b(4, 1)
    ag_b(7, 1)
    rs_near(2)
    ag_b(3, 0)
    ag_b_far(1)
    rs_late(2)
    ag_b(1, 1)
    sibling_terms(3)
    rs_late(1)
    rs_near(1)
    ag_b_far(3)
    ag_b_far(2)
    rs_far(5)
    rs_near(4)
    rs_a_far(0)
    ag_b(0, 1)
    ag_b(6, 0)
    ag_b_far(5)
    rs_late(4)
    ag_b_far(6)
    ag_b_far(0)
    ag_b(5, 0)
    rs_far(7)
    rs_far(6)
    rs_near(3)
    ag_b_far(4)
    rs_late(3)
    ag_b_far(7)
    rs_near(5)
    rs_near(6)
    ag_b(7, 0)
    ag_sibling()
    backward_tap(2)
    backward_tap(0)
    backward_tap(6)
    backward_tap(7)
    backward_tap(3)
    rs_a_late(0)
    backward_tap(1)
    rs_a_near(0)
    backward_tap(5)
    backward_tap(8)
    backward_tap(4)
    rs_late(5)
    backward_rest(0)
    rs_a_far(1)
    rs_late(6)
    backward_rest(1)
    norm_start(0, ncol[...].T[:8])
    rs_other_plane()
    rs_near(7)
    rs_late(7)
    rs_a_near(1)
    rs_a_late(1)
    norm_start(1, norm_sum(0))
    rs_own_plane()
    forward(0, 2)
    norm_partner_start()
    forward(2, 4)
    write_input_grad()
    forward(4, 6)
    forward(6, 8)

    for copy in sent:
        copy.wait_send()
    for i in range(8):
        sib_copy(i).wait_send()
        b2_copy(i).wait_send()
        for way in range(2):
            b1_copy(i, way).wait_send()
    for h in range(2):
        a2_copy(h).wait_send()
        for way in range(2):
            a1_copy(h, way).wait_send()

    rs_partner()
    norm_last()

    z_copy.wait_send()
    for copy in p_copies + n3_copies:
        copy.wait_send()
    for stage in range(2):
        for d in range(1, 8):
            norm_copy(stage, d, True).wait_send()


def finish(*refs):
    for source, target in zip(refs[: len(refs) // 2], refs[len(refs) // 2 :]):
        target[...] = source[...]


def shards(latents, cotangent, conv_weight, norm_gain, norm_shift, partner_bit):
    chans = latents.shape[3]
    shard = conv_weight.shape[1]
    count = lax.axis_size("fsdp")
    vmem = pl.BlockSpec(memory_space=pltpu.VMEM)
    anywhere = pl.BlockSpec(memory_space=pl.ANY)
    piece = (SLAB, chans)
    dma = pltpu.SemaphoreType.DMA
    results = pl.pallas_call(
        kernel,
        out_shape=(
            jax.ShapeDtypeStruct((POS, chans), BF),
            jax.ShapeDtypeStruct((POS, chans), BF),
            jax.ShapeDtypeStruct((shard, 1, chans), F32),
            jax.ShapeDtypeStruct((2, chans), F32),
        ),
        in_specs=[anywhere] * 3 + [vmem] * 2 + [pl.BlockSpec(memory_space=pltpu.SMEM)],
        out_specs=(vmem,) * 4,
        scratch_shapes=[
            pltpu.VMEM((POS, chans), BF),
            pltpu.VMEM((POS, chans), BF),
            pltpu.VMEM((shard, chans), BF),
            pltpu.VMEM((count, *piece), BF),
            pltpu.VMEM((count, SLAB, POS), BF),
            pltpu.VMEM((count * shard + 8, POS), F32),
            pltpu.VMEM((9, chans, POS), BF),
            pltpu.VMEM((8, 4, *piece), F32),
            pltpu.VMEM((4, chans + 2 * SLAB, POS), F32),
            *[pltpu.VMEM((chans, POS), F32)] * 3,
            pltpu.VMEM((POS, chans), F32),
            *[pltpu.VMEM((chans, 128), F32)] * 4,
            pltpu.VMEM(piece, F32),
            *[pltpu.VMEM((8, 4, *piece), BF)] * 2,
            *[pltpu.VMEM((8, *piece), BF)] * 2,
            *[pltpu.VMEM((8, 2, *piece), BF)] * 2,
            *[pltpu.VMEM((2, *piece), BF)] * 2,
            *[pltpu.VMEM((2, 2, *piece), BF)] * 2,
            *[pltpu.VMEM(piece, BF)] * 2,
            pltpu.VMEM(piece, BF),
            pltpu.VMEM((2, *piece), BF),
            *[pltpu.VMEM((8, chans), F32), pltpu.VMEM((8, 8, chans), F32)] * 2,
            pltpu.VMEM((8, chans), F32),
            pltpu.VMEM((2, 8, chans), F32),
            dma((count,)), dma((count,)),
            dma((8,)), dma((8,)),
            dma((8,)), dma((8,)),
            dma((8, 2)), dma((8, 2)),
            dma((2,)), dma((2,)),
            dma((2, 2)), dma((2, 2)),
            dma, dma,
            dma((2,)), dma((2,)),
            dma((8,)), dma((8,)), dma((8,)), dma((8,)),
            dma((2,)), dma((2,)), dma((3,)),
        ],
        compiler_params=pltpu.CompilerParams(
            collective_id=0, has_side_effects=True, vmem_limit_bytes=60 << 20
        ),
        name="block",
    )(
        latents.reshape(POS, chans), cotangent.reshape(POS, chans), conv_weight[0],
        norm_gain, norm_shift, partner_bit,
    )
    block_out, input_grad, weight_grad, norm_grad = pl.pallas_call(
        finish,
        out_shape=[jax.ShapeDtypeStruct(result.shape, result.dtype) for result in results],
        in_specs=[vmem] * 4,
        out_specs=[vmem] * 4,
        name="finish",
    )(*results)
    return (
        block_out.reshape(latents.shape),
        input_grad.reshape(latents.shape),
        weight_grad.reshape(1, shard, chans),
        norm_grad[None],
    )


def solution(mesh):
    in_specs = (
        P(("rep", "fsdp"), None, None, None),
        P(("rep", "fsdp"), None, None, None),
        P("rep", "fsdp", None),
        P("rep", None),
        P("rep", None),
        P(),
    )
    out_specs = (
        P(("rep", "fsdp"), None, None, None),
        P(("rep", "fsdp"), None, None, None),
        P("rep", "fsdp", None),
        P("rep", None, None),
    )
    return jax.shard_map(shards, mesh=mesh, in_specs=in_specs, out_specs=out_specs, check_vma=False)
```

```python
import jax
import jax.numpy as jnp
from jax import lax
from jax.experimental import pallas as pl
from jax.experimental.pallas import tpu as pltpu
from jax.sharding import PartitionSpec as P

GROUPS = 32
SIDE = 16
POS = SIDE * SIDE
SLAB = 96
UNROLL = 4
BF = jnp.bfloat16
F32 = jnp.float32
TAPS = [(a - 1, b - 1) for a in range(3) for b in range(3)]


def order(step):
    return (step + (step // 2) * (1 - 2 * (step % 2)) + 2) % 4


def lane_mask(down, right):
    lane = lax.broadcasted_iota(jnp.int32, (1, POS), 1)
    row, col = lane // SIDE + down, lane % SIDE + right
    return (row >= 0) & (row < SIDE) & (col >= 0) & (col < SIDE)


def kernel(
    lat_in, cot_in, w_in, gain, shift, bits, out, in_grad, w_grad, n_grad,
    lat, cot, w_own, wg, pt, tall, cs, tm, bacc, xt, nt, at, acc, gcol, scol, rcol, ncol, fin,
    sib_s, sib_r, b2_s, b2_r, b1_s, b1_r, a2_s, a2_r, a1_s, a1_r, z_s, z_r, p_s, p_r,
    n1_s, n1_r, n2_s, n2_r, n3_s, n3_r,
    ag_ss, ag_rs, sib_ss, sib_rs, b2_ss, b2_rs, b1_ss, b1_rs, a2_ss, a2_rs, a1_ss, a1_rs,
    z_ss, z_rs, p_ss, p_rs, n1_ss, n1_rs, n2_ss, n2_rs, n3_ss, n3_rs, in_s,
):
    chans = lat.shape[1]
    shard = w_in.shape[0]
    count = wg.shape[0]
    krows = count * shard
    rep, fs = lax.axis_index("rep"), lax.axis_index("fsdp")
    x, z, y, core = fs // 16, (fs // 8) % 2, (fs // 2) % 4, fs % 2
    a, b = x + (y - x) * core, y + (x - y) * core

    def slot(a_, z_, b_, core_):
        return (a_ % 4) * (16 - 14 * core_) + z_ * 8 + (b_ % 4) * (2 + 14 * core_) + core_

    def at_ab(da, db):
        return (rep, slot(a + da, z, b + db, core))

    sibling = (rep, fs + 1 - 2 * core)
    opposite = (rep, slot(a, 1 - z, b, core))
    partners = ((rep + 1 - 2 * (rep % 2), fs), (rep + 2 - 4 * (rep // 2), fs))

    def remote(src, dst, send_sem, recv_sem, device):
        return pltpu.make_async_remote_copy(
            src_ref=src, dst_ref=dst, send_sem=send_sem, recv_sem=recv_sem,
            device_id=device, device_id_type=pl.DeviceIdType.MESH,
        )

    sent = []

    def ag_send(index, *devices):
        for device in devices:
            copy = remote(wg.at[index], wg.at[index], ag_ss.at[len(sent)], ag_rs.at[index], device)
            copy.start()
            sent.append(copy)

    def ag_wait(index):
        remote(wg.at[index], wg.at[index], ag_ss.at[0], ag_rs.at[index], sibling).wait_recv()

    b_both = (at_ab(0, 1), at_ab(0, 3))
    a_both = (at_ab(1, 0), at_ab(3, 0))
    def of_plane(other):
        return 1 - z if other else z

    arrivals = [(0, 0), (3, 0), (1, 0), (0, 1), (2, 0), (3, 1), (1, 1), (2, 1)]

    def ag_first():
        ag_send(fs, opposite, *a_both, *b_both, sibling)

    def ag_near(other, side):
        zz, step = of_plane(other), 3 + 2 * (z + side)
        own = slot(a + step, zz, b, core)
        ag_wait(own)
        if other == side:
            ag_send(own, at_ab(1 + 2 * zz, 0))
        ag_send(own, *b_both, sibling)

    def ag_opposite():
        own = slot(a, 1 - z, b, core)
        ag_wait(own)
        ag_send(own, *a_both, *b_both, sibling)

    def ag_far(other):
        own = slot(a + 2, of_plane(other), b, core)
        ag_wait(own)
        ag_send(own, *b_both, sibling)

    def ag_b(k, side):
        da, other = arrivals[k]
        zz = of_plane(other)
        own = slot(a + da, zz, b + 3 + 2 * (z + side), core)
        ag_wait(own)
        if other == side:
            ag_send(own, at_ab(0, 1 + 2 * zz))
        ag_send(own, sibling)

    def ag_b_far(k):
        da, other = arrivals[k]
        own = slot(a + da, of_plane(other), b + 2, core)
        ag_wait(own)
        ag_send(own, sibling)

    def ag_sibling():
        def body(step, carry):
            ag_wait(2 * step + 1 - core)
            return carry

        lax.fori_loop(0, count // 2, body, 0)

    def plane(i):
        return z + (1 - 2 * z) * (1 - i // 4)

    def terms(first, indices):
        lhs = jnp.concatenate([pt[index] for index in indices], axis=0)
        return jnp.dot(lhs, cot[...], preferred_element_type=F32)

    def sib_copy(i):
        return remote(sib_s.at[i], sib_r.at[i], sib_ss.at[i], sib_rs.at[i], sibling)

    def sibling_terms(g):
        todo = [(i, jb) for i in (2 * g, 2 * g + 1) for jb in range(4)]
        value = terms(g, [slot(b + order(i % 4), plane(i), a + order(jb), 1 - core) for i, jb in todo])
        for n, (i, jb) in enumerate(todo):
            sib_s[i, jb] = value[n * SLAB : (n + 1) * SLAB].astype(BF)
            if jb == 3:
                sib_copy(i).start()

    def own_terms(g):
        todo = [(i, jb) for i in (2 * g, 2 * g + 1) for jb in range(4)]
        value = terms(g, [slot(a + order(i % 4), plane(i), b + order(jb), core) for i, jb in todo])
        for n, (i, jb) in enumerate(todo):
            tm[i, jb] = value[n * SLAB : (n + 1) * SLAB]

    def chip_term(i, jb):
        return tm[i, jb] + sib_r[i, jb].astype(F32)

    def b2_copy(i):
        return remote(b2_s.at[i], b2_r.at[i], b2_ss.at[i], b2_rs.at[i], at_ab(0, 1 + 2 * (i % 2)))

    def b1_copy(i, way):
        return remote(
            b1_s.at[i, way], b1_r.at[i, way], b1_ss.at[i, way], b1_rs.at[i, way],
            at_ab(0, 1 + 2 * way),
        )

    def rs_far(i):
        sib_copy(i).wait_recv()
        b2_s[i] = chip_term(i, 0).astype(BF)
        b2_copy(i).start()

    def rs_near(i):
        way = 1 - i % 2
        b1_s[i, way] = chip_term(i, 2 - way).astype(BF)
        b1_copy(i, way).start()

    def rs_late(i):
        way = i % 2
        b2_copy(i).wait_recv()
        b1_s[i, way] = (chip_term(i, 2 - way) + b2_r[i].astype(F32)).astype(BF)
        b1_copy(i, way).start()

    def row_term(i):
        for way in range(2):
            b1_copy(i, way).wait_recv()
        return chip_term(i, 3) + b1_r[i, 0].astype(F32) + b1_r[i, 1].astype(F32)

    def a2_copy(h):
        return remote(a2_s.at[h], a2_r.at[h], a2_ss.at[h], a2_rs.at[h], at_ab(1 + 2 * h, 0))

    def a1_copy(h, way):
        return remote(
            a1_s.at[h, way], a1_r.at[h, way], a1_ss.at[h, way], a1_rs.at[h, way],
            at_ab(1 + 2 * way, 0),
        )

    def rs_a_far(h):
        a2_s[h] = row_term(4 * h).astype(BF)
        a2_copy(h).start()

    def rs_a_near(h):
        way = 1 - h
        a1_s[h, way] = row_term(4 * h + 2 - way).astype(BF)
        a1_copy(h, way).start()

    def rs_a_late(h):
        way = h
        value = row_term(4 * h + 2 - way)
        a2_copy(h).wait_recv()
        a1_s[h, way] = (value + a2_r[h].astype(F32)).astype(BF)
        a1_copy(h, way).start()

    def plane_term(h):
        value = row_term(4 * h + 3)
        for way in range(2):
            a1_copy(h, way).wait_recv()
        return value + a1_r[h, 0].astype(F32) + a1_r[h, 1].astype(F32)

    z_copy = remote(z_s, z_r, z_ss, z_rs, opposite)
    p_copies = [remote(p_s, p_r.at[i], p_ss.at[i], p_rs.at[i], partners[i]) for i in range(2)]

    def rs_other_plane():
        z_s[...] = plane_term(0).astype(BF)
        z_copy.start()

    def rs_own_plane():
        value = plane_term(1)
        z_copy.wait_recv()
        value = value + z_r[...].astype(F32)
        fin[...] = value
        p_s[...] = value.astype(BF)
        for copy in p_copies:
            copy.start()

    def picked(index, first, second):
        second_share = bits[index].astype(F32)
        return first * (1.0 - second_share) + second * second_share

    def rs_partner():
        for copy in p_copies:
            copy.wait_recv()
        other = picked(fs, p_r[0].astype(F32), p_r[1].astype(F32))
        w_grad[...] = ((fin[...] + other) * (0.5 / count))[:shard].reshape(w_grad.shape)

    me1, me2 = x * 2 + core, z * 4 + y

    def peer1(d):
        other = (me1 + d) % 8
        return other, (rep, (other // 2) * 16 + z * 8 + y * 2 + other % 2)

    def peer2(d):
        other = (me2 + d) % 8
        return other, (rep, x * 16 + (other // 4) * 8 + (other % 4) * 2 + core)

    norm_stages = [(n1_s, n1_r, n1_ss, n1_rs, me1, peer1), (n2_s, n2_r, n2_ss, n2_rs, me2, peer2)]

    def norm_copy(stage, d, mine):
        send, recv, send_sems, recv_sems, me, peer = norm_stages[stage]
        other, device = peer(d)
        index = me if mine else other
        return remote(send, recv.at[index], send_sems.at[d], recv_sems.at[index], device)

    def norm_start(stage, value):
        send, recv, _, _, me, _ = norm_stages[stage]
        send[...] = value
        recv[me] = value
        for d in range(1, 8):
            norm_copy(stage, d, True).start()

    def norm_sum(stage):
        for d in range(1, 8):
            norm_copy(stage, d, False).wait_recv()
        recv = norm_stages[stage][1]
        total = recv[0]
        for i in range(1, 8):
            total = total + recv[i]
        return total

    n3_copies = [remote(n3_s, n3_r.at[i], n3_ss.at[i], n3_rs.at[i], partners[i]) for i in range(2)]

    def norm_partner_start():
        n3_s[...] = norm_sum(1)
        for copy in n3_copies:
            copy.start()

    def norm_last():
        for copy in n3_copies:
            copy.wait_recv()
        other = picked(0, n3_r[0], n3_r[1])
        n_grad[...] = ((n3_s[...] + other) * (0.5 / count))[:2]

    block = 40
    half = block // 2
    blocks = chans // block
    width = float(POS * (chans // GROUPS))

    def group_mean(column):
        first = lax.broadcasted_iota(jnp.int32, (block, 1), 0) < half
        low = jnp.sum(jnp.where(first, column, 0.0), axis=0, keepdims=True)
        high = jnp.sum(jnp.where(first, 0.0, column), axis=0, keepdims=True)
        return jnp.where(first, low, high) / width

    def to_columns(row):
        return jnp.broadcast_to(row, (128, chans)).T

    def transposes():
        gcol[...] = to_columns(gain[...])
        scol[...] = to_columns(shift[...])
        for i in range(chans // 128):
            span = slice(i * 128, (i + 1) * 128)
            xt[span, :] = lat[:, span].astype(F32).T

    def norm_forward():
        def body(i, carry):
            for u in range(UNROLL):
                span = pl.ds(pl.multiple_of((i * UNROLL + u) * block, block), block)
                values = xt[span, :]
                centered = values - group_mean(jnp.sum(values, axis=1, keepdims=True))
                spread = group_mean(jnp.sum(centered * centered, axis=1, keepdims=True))
                scale = lax.rsqrt(spread + 1e-5)
                normed = centered * scale
                pre = normed * gcol[span, :1] + scol[span, :1]
                nt[span, :] = normed
                rcol[span, :] = jnp.broadcast_to(scale, (block, 128))
                at[span, :] = pre / (1.0 + jnp.exp(-pre))
            return carry

        lax.fori_loop(0, blocks // UNROLL, body, 0)

    def make_patches():
        tall[krows:, :] = jnp.zeros((8, POS), F32)

        def taps(i, carry):
            start = pl.multiple_of(i * 80, 80)
            values = at[pl.ds(start, 80), :]
            for t, (down, right) in enumerate(TAPS):
                offset = 16 * down + right
                moved = values if offset == 0 else pltpu.roll(values, -offset % POS, 1)
                tall[pl.ds(t * chans + start, 80), :] = jnp.where(lane_mask(down, right), moved, 0.0)
            return carry

        lax.fori_loop(0, chans // 80, taps, 0)
        keep = lax.broadcasted_iota(jnp.int32, (SLAB, 1), 0) < shard

        def slabs(g, carry):
            for j in range(4):
                base, rest = j * shard // 8 * 8, j * shard % 8
                start = pl.multiple_of(g * (4 * shard) + base, 8)
                if rest:
                    values = pltpu.roll(tall[pl.ds(start, SLAB + 8), :], SLAB + 8 - rest, 0)[:SLAB]
                else:
                    values = tall[pl.ds(start, SLAB), :]
                pt[g * 4 + j] = jnp.where(keep, values, 0.0).astype(BF)
            return carry

        lax.fori_loop(0, count // 4, slabs, 0)

    def cotangent_shifts():
        for i in range(chans // 128):
            span = slice(i * 128, (i + 1) * 128)
            at[span, :] = cot[:, span].astype(F32).T

        def taps(i, carry):
            span = pl.ds(pl.multiple_of(i * 80, 80), 80)
            values = at[span, :]
            for t, (down, right) in enumerate(TAPS):
                offset = 16 * down + right
                moved = values if offset == 0 else pltpu.roll(values, offset % POS, 1)
                cs[t, span, :] = jnp.where(lane_mask(-down, -right), moved, 0.0).astype(BF)
            return carry

        lax.fori_loop(0, chans // 80, taps, 0)
        bacc[...] = jnp.zeros_like(bacc)

    def forward(first, last):
        def body(g, carry):
            group = pl.ds(g * 8, 8)
            acc[...] += lax.dot_general(
                pt[group].reshape(8 * SLAB, POS), wg[group].reshape(8 * SLAB, chans),
                (((0,), (0,)), ((), ())), preferred_element_type=F32,
            )
            return carry

        if first == 0:
            acc[...] = jnp.zeros_like(acc)
        lax.fori_loop(first, last, body, 0)
        if last == count // 8:
            out[...] = acc[...].astype(BF)

    def backward_tap(t):
        low = chans * t // shard
        slabs = (chans * t + chans - 1) // shard - low + 1
        grads = jnp.dot(
            wg[low : low + slabs].reshape(slabs * SLAB, chans), cs[t], preferred_element_type=F32
        )
        for j in range(slabs):
            first = shard * (low + j) - chans * t
            rest = first % 8
            start = SLAB + first - rest
            bacc[rest // 2, start : start + SLAB, :] += grads[j * SLAB : (j + 1) * SLAB]

    def backward_rest(part):
        lane = lax.broadcasted_iota(jnp.int32, (1, 128), 1)

        def one(i):
            start = pl.multiple_of(i * block, block)
            span = pl.ds(start, block)
            act_grad = bacc[0, pl.ds(start + SLAB, block), :]
            for r in (2, 4, 6):
                window = bacc[r // 2, pl.ds(start + SLAB - 8, block + 8), :]
                act_grad += pltpu.roll(window, block + r, 0)[:block]
            normed, gain_col = nt[span, :], gcol[span, :1]
            pre = normed * gain_col + scol[span, :1]
            sigma = 1.0 / (1.0 + jnp.exp(-pre))
            pre_grad = act_grad * sigma * (1.0 + pre * (1.0 - sigma))
            gain_grad = jnp.sum(pre_grad * normed, axis=1, keepdims=True)
            shift_grad = jnp.sum(pre_grad, axis=1, keepdims=True)
            ncol[span, :] = jnp.where(lane == 0, gain_grad, jnp.where(lane == 1, shift_grad, 0.0))
            first = group_mean(shift_grad * gain_col)
            second = group_mean(gain_grad * gain_col)
            xt[span, :] = rcol[span, :1] * (pre_grad * gain_col - first - normed * second)

        def body(i, carry):
            for u in range(UNROLL):
                one(i * UNROLL + u)
            return carry

        steps = blocks // UNROLL // 2
        lax.fori_loop(part * steps, (part + 1) * steps, body, 0)

    def write_input_grad():
        for i in range(chans // 128):
            span = slice(i * 128, (i + 1) * 128)
            in_grad[:, span] = xt[span, :].T.astype(BF)

    barrier = pltpu.get_barrier_semaphore()
    neighbours = [peer(d)[1] for peer in (peer1, peer2) for d in range(1, 8)] + list(partners)
    for device in neighbours:
        pl.semaphore_signal(barrier, inc=1, device_id=device, device_id_type=pl.DeviceIdType.MESH)
    arriving = [
        pltpu.make_async_copy(source, target, in_s.at[i])
        for i, (source, target) in enumerate(((w_in, w_own), (lat_in, lat), (cot_in, cot)))
    ]
    for copy in arriving:
        copy.start()
    wg[fs, SLAB - 16 :, :] = jnp.zeros((16, chans), BF)
    arriving[0].wait()
    wg[fs, :shard, :] = w_own[...]
    pl.semaphore_wait(barrier, len(neighbours))

    ag_first()
    arriving[1].wait()
    transposes()
    arriving[2].wait()
    norm_forward()
    make_patches()
    ag_near(0, 0)
    own_terms(1)
    ag_opposite()
    sibling_terms(0)
    ag_near(0, 1)
    own_terms(0)
    own_terms(2)
    rs_far(0)
    sibling_terms(1)
    rs_near(0)
    ag_far(0)
    rs_far(2)
    sibling_terms(2)
    rs_far(1)
    sibling_terms(3)
    ag_near(1, 1)
    ag_near(1, 0)
    rs_late(0)
    rs_far(4)
    ag_b(2, 0)
    ag_b(2, 1)
    ag_b(3, 1)
    ag_b(0, 1)
    ag_b(0, 0)
    ag_b(1, 0)
    ag_b(4, 0)
    ag_far(1)
    ag_b(6, 1)
    ag_b(5, 0)
    rs_far(3)
    rs_late(2)
    own_terms(3)
    ag_b(4, 1)
    ag_b(5, 1)
    ag_b(3, 0)
    cotangent_shifts()
    ag_b(1, 1)
    ag_b(7, 1)
    rs_near(2)
    ag_b_far(2)
    rs_late(1)
    rs_far(5)
    ag_b_far(0)
    rs_a_far(0)
    rs_near(1)
    rs_late(4)
    rs_far(7)
    rs_far(6)
    ag_b(6, 0)
    ag_b_far(3)
    rs_near(4)
    ag_b_far(6)
    ag_b_far(5)
    rs_late(3)
    ag_b_far(1)
    ag_b_far(4)
    rs_near(3)
    ag_b_far(7)
    rs_near(5)
    rs_near(6)
    ag_b(7, 0)
    ag_sibling()
    backward_tap(6)
    backward_tap(0)
    backward_tap(4)
    backward_tap(3)
    backward_tap(2)
    rs_a_late(0)
    backward_tap(1)
    rs_a_near(0)
    backward_tap(8)
    backward_tap(5)
    backward_tap(7)
    rs_late(5)
    backward_rest(1)
    rs_a_far(1)
    rs_late(6)
    backward_rest(0)
    norm_start(0, ncol[...].T[:8])
    rs_other_plane()
    rs_near(7)
    rs_late(7)
    rs_a_near(1)
    rs_a_late(1)
    norm_start(1, norm_sum(0))
    rs_own_plane()
    norm_partner_start()
    write_input_grad()
    forward(0, 2)
    forward(2, 4)
    forward(4, 6)
    forward(6, 8)

    for copy in sent:
        copy.wait_send()
    for i in range(8):
        sib_copy(i).wait_send()
        b2_copy(i).wait_send()
        for way in range(2):
            b1_copy(i, way).wait_send()
    for h in range(2):
        a2_copy(h).wait_send()
        for way in range(2):
            a1_copy(h, way).wait_send()

    rs_partner()
    norm_last()

    z_copy.wait_send()
    for copy in p_copies + n3_copies:
        copy.wait_send()
    for stage in range(2):
        for d in range(1, 8):
            norm_copy(stage, d, True).wait_send()


def finish(*refs):
    for source, target in zip(refs[: len(refs) // 2], refs[len(refs) // 2 :]):
        target[...] = source[...]


def shards(latents, cotangent, conv_weight, norm_gain, norm_shift, partner_bit):
    chans = latents.shape[3]
    shard = conv_weight.shape[1]
    count = lax.axis_size("fsdp")
    vmem = pl.BlockSpec(memory_space=pltpu.VMEM)
    anywhere = pl.BlockSpec(memory_space=pl.ANY)
    piece = (SLAB, chans)
    dma = pltpu.SemaphoreType.DMA
    results = pl.pallas_call(
        kernel,
        out_shape=(
            jax.ShapeDtypeStruct((POS, chans), BF),
            jax.ShapeDtypeStruct((POS, chans), BF),
            jax.ShapeDtypeStruct((shard, 1, chans), F32),
            jax.ShapeDtypeStruct((2, chans), F32),
        ),
        in_specs=[anywhere] * 3 + [vmem] * 2 + [pl.BlockSpec(memory_space=pltpu.SMEM)],
        out_specs=(vmem,) * 4,
        scratch_shapes=[
            pltpu.VMEM((POS, chans), BF),
            pltpu.VMEM((POS, chans), BF),
            pltpu.VMEM((shard, chans), BF),
            pltpu.VMEM((count, *piece), BF),
            pltpu.VMEM((count, SLAB, POS), BF),
            pltpu.VMEM((count * shard + 8, POS), F32),
            pltpu.VMEM((9, chans, POS), BF),
            pltpu.VMEM((8, 4, *piece), F32),
            pltpu.VMEM((4, chans + 2 * SLAB, POS), F32),
            *[pltpu.VMEM((chans, POS), F32)] * 3,
            pltpu.VMEM((POS, chans), F32),
            *[pltpu.VMEM((chans, 128), F32)] * 4,
            pltpu.VMEM(piece, F32),
            *[pltpu.VMEM((8, 4, *piece), BF)] * 2,
            *[pltpu.VMEM((8, *piece), BF)] * 2,
            *[pltpu.VMEM((8, 2, *piece), BF)] * 2,
            *[pltpu.VMEM((2, *piece), BF)] * 2,
            *[pltpu.VMEM((2, 2, *piece), BF)] * 2,
            *[pltpu.VMEM(piece, BF)] * 2,
            pltpu.VMEM(piece, BF),
            pltpu.VMEM((2, *piece), BF),
            *[pltpu.VMEM((8, chans), F32), pltpu.VMEM((8, 8, chans), F32)] * 2,
            pltpu.VMEM((8, chans), F32),
            pltpu.VMEM((2, 8, chans), F32),
            dma((count,)), dma((count,)),
            dma((8,)), dma((8,)),
            dma((8,)), dma((8,)),
            dma((8, 2)), dma((8, 2)),
            dma((2,)), dma((2,)),
            dma((2, 2)), dma((2, 2)),
            dma, dma,
            dma((2,)), dma((2,)),
            dma((8,)), dma((8,)), dma((8,)), dma((8,)),
            dma((2,)), dma((2,)), dma((3,)),
        ],
        compiler_params=pltpu.CompilerParams(
            collective_id=0, has_side_effects=True, vmem_limit_bytes=60 << 20
        ),
        name="block",
    )(
        latents.reshape(POS, chans), cotangent.reshape(POS, chans), conv_weight[0],
        norm_gain, norm_shift, partner_bit,
    )
    block_out, input_grad, weight_grad, norm_grad = pl.pallas_call(
        finish,
        out_shape=[jax.ShapeDtypeStruct(result.shape, result.dtype) for result in results],
        in_specs=[vmem] * 4,
        out_specs=[vmem] * 4,
        name="finish",
    )(*results)
    return (
        block_out.reshape(latents.shape),
        input_grad.reshape(latents.shape),
        weight_grad.reshape(1, shard, chans),
        norm_grad[None],
    )


def solution(mesh):
    in_specs = (
        P(("rep", "fsdp"), None, None, None),
        P(("rep", "fsdp"), None, None, None),
        P("rep", "fsdp", None),
        P("rep", None),
        P("rep", None),
        P(),
    )
    out_specs = (
        P(("rep", "fsdp"), None, None, None),
        P(("rep", "fsdp"), None, None, None),
        P("rep", "fsdp", None),
        P("rep", None, None),
    )
    return jax.shard_map(shards, mesh=mesh, in_specs=in_specs, out_specs=out_specs, check_vma=False)
```
